32 devices in a mesh: groups: 2 (over x), ctx: 8 (over z, y), head: 2 (over core).
Axes of the slice: x: 2, y: 2, z: 4, core: 2. Of those that a mesh axis runs over, the one named last changes fastest.
Arguments:
- query_rows: bfloat16 [4096, 2048], P(('groups', 'ctx'), 'head'), parts along dimension 0, may hold values from -6 to 6
- key_rows: bfloat16 [4096, 256], P(('groups', 'ctx'), 'head'), parts along dimension 0, may hold values from -6 to 6
- value_rows: bfloat16 [4096, 256], P(('groups', 'ctx'), 'head'), parts along dimension 0, may hold values from -6 to 6
- out_grad: bfloat16 [4096, 2048], P(('groups', 'ctx'), 'head'), parts along dimension 0, may hold values from -6 to 6
- doc_lengths: int32 [32], P('groups'), parts along dimension 0, may hold values from 1 to 256, 2048 in all
Outputs:
- attended: bfloat16 [4096, 2048], P(('groups', 'ctx'), 'head'), parts along dimension 0
- query_grad: bfloat16 [4096, 2048], P(('groups', 'ctx'), 'head'), parts along dimension 0
- key_grad: bfloat16 [4096, 256], P(('groups', 'ctx'), 'head'), parts along dimension 0
- value_grad: bfloat16 [4096, 256], P(('groups', 'ctx'), 'head'), parts along dimension 0
The draws below stay inside these ranges and needn't reach their ends.
There are 2 independent parts, one for each index of `groups`. The reference program is written for one: setup_inputs(seed, part) draws one part's arguments, and reference() takes and returns one part's arrays. A program takes and returns all parts, laid end to end along the dimension named above; each array names one. Nothing has to cross between parts.
Inputs may be any that keep to these rules, and one draw needn't show every extreme that they name: `doc_lengths`: documents are laid end to end in position order and their lengths sum to 2048; the longest has exactly 256 tokens.
All inputs are finite; a program needn't handle non-finite values.
Results may differ from the reference program's by a relative error of at most 0.017.
Values may be sent and summed in bfloat16 or wider, within the bound.
No kernel may reach another device: no remote copies, remote signals or barrier semaphores. Data moves between devices by JAX's collectives and lax.ppermute only.
A program may use at most 64 MiB of HBM per device.

```python
import math
import jax
import jax.numpy as jnp
import numpy as np
from jax import lax

HEADS = 16
KV_HEADS = 2
HEAD_DIM = 128
TOK_DEV = 256
STRETCH = 128
TOKENS = 2048
DOCMAX = 256
NDOCS = 16
N_CTX = 8


def rough_entries(key, row_total, col_total):
    entries = jax.random.normal(jax.random.fold_in(key, 1), (row_total, col_total), jnp.float32)
    return jnp.clip(entries, -6.0, 6.0)


def draw_query_rows(key, part):
    own_key = jax.random.fold_in(key, 101)
    entries = rough_entries(own_key, TOKENS, HEADS * HEAD_DIM)
    return entries.astype(jnp.bfloat16)


def draw_key_rows(key, part):
    own_key = jax.random.fold_in(key, 202)
    entries = rough_entries(own_key, TOKENS, KV_HEADS * HEAD_DIM)
    return entries.astype(jnp.bfloat16)


def block_scale(stream_key, extent, split, least, high):
    gain = 1.0
    for dim, parts in split:
        draws = jax.random.uniform(jax.random.fold_in(jax.random.fold_in(stream_key, 6), dim), (parts,), jnp.float32, least / len(split), high / len(split))
        gain = gain * jnp.repeat(jnp.exp(draws), extent[dim] // parts).reshape((-1,) + (1,) * (len(extent) - 1 - dim))
    return gain


def length_profile(amount, total, reach, skew):
    loads = [(1 << 20) // math.isqrt(rank ** skew) + 1 for rank in range(2, amount + 1)]
    surplus, counts = total - reach - (amount - 1), [1] * (amount - 1)
    while surplus > 0:
        free = [i for i in range(amount - 1) if counts[i] < reach]
        whole, remaining = sum([loads[i] for i in free]), surplus
        for i in free:
            extra = min(reach - counts[i], max(1, remaining * loads[i] // whole), surplus)
            counts[i] = counts[i] + extra
            surplus = surplus - extra
    return np.array([reach] + counts)


def ragged(rng, number_of, total, most, skew):
    if number_of == 2:
        one = jax.random.randint(rng, (), max(1, total - most), min(most, total - 1) + 1)
        return jnp.stack([one, total - one])
    tallies = jnp.asarray(length_profile(number_of, total, most, skew), jnp.int32)
    couples = (number_of - 1) // 2
    donor, sink = tallies[1:1 + 2 * couples:2], tallies[2:2 + 2 * couples:2]
    slack = jnp.minimum(donor - 1, most - sink)
    passed = jax.random.randint(jax.random.fold_in(rng, 1), (couples,), 0, 1 << 20) % (slack + 1)
    tallies = tallies.at[1:1 + 2 * couples:2].set(donor - passed).at[2:2 + 2 * couples:2].set(sink + passed)
    return tallies[jax.random.permutation(jax.random.fold_in(rng, 2), number_of)]


def centred(key, shape, deviation, most, pieces=(), kind=jnp.bfloat16):
    values = jax.random.normal(key, shape, jnp.float32) * deviation
    if len(pieces) > 0:
        values = block_scale(key, shape, pieces, -0.22, 0.18) * values
    return jnp.clip(values, min=-most, max=most).astype(kind)


def setup_inputs(seed: int = 0, part: int = 0) -> dict:
    key_list = jax.random.split(jax.random.key(seed), 6)
    part_splits = jax.random.split(jax.random.fold_in(key_list[5], part), 6)
    query_rows = draw_query_rows(jax.random.fold_in(jax.random.fold_in(key_list[5], part), 71), part)
    key_rows = draw_key_rows(jax.random.fold_in(jax.random.fold_in(key_list[5], part), 71), part)
    value_rows = centred(part_splits[2], (TOKENS, KV_HEADS * HEAD_DIM), 1.0, 6.0, ((0, 8), (1, 2)))
    out_grad = centred(part_splits[3], (TOKENS, HEADS * HEAD_DIM), 1.0, 6.0, ((0, 8), (1, 2)))
    doc_lengths = ragged(part_splits[4], NDOCS, TOKENS, DOCMAX, 2).astype(jnp.int32)
    return dict(query_rows=query_rows, key_rows=key_rows, value_rows=value_rows, out_grad=out_grad, doc_lengths=doc_lengths)


def row_positions(row_total, stretch_len, ctx_count):
    row_index = jnp.arange(row_total, dtype=jnp.int32)
    device = row_index // (2 * stretch_len)
    upper_half = (row_index // stretch_len) % 2
    stretch_id = jnp.where(upper_half == 0, device, 2 * ctx_count - 1 - device)
    return (stretch_id * stretch_len + row_index % stretch_len).astype(jnp.int32)


def position_rows(row_total, stretch_len, ctx_count):
    position = jnp.arange(row_total, dtype=jnp.int32)
    stretch_id = position // stretch_len
    device = jnp.where(stretch_id < ctx_count, stretch_id, 2 * ctx_count - 1 - stretch_id)
    upper_half = jnp.where(stretch_id < ctx_count, 0, 1)
    return (device * 2 * stretch_len + upper_half * stretch_len + position % stretch_len).astype(jnp.int32)


def documents(positions, doc_lengths):
    starts = jnp.cumsum(doc_lengths) - doc_lengths
    return (jnp.sum((starts[None, :] <= positions[:, None]).astype(jnp.int32), axis=1) - 1).astype(jnp.int32)


def settle(entries):
    return lax.optimization_barrier(entries.astype(jnp.bfloat16)).astype(jnp.float32)


def reference(query_rows, key_rows, value_rows, out_grad, doc_lengths):
    group_size = HEADS // KV_HEADS
    scaling = HEAD_DIM ** -0.5
    block_len = TOK_DEV
    span_len = DOCMAX + block_len
    order = position_rows(TOKENS, STRETCH, N_CTX)
    inverse = row_positions(TOKENS, STRETCH, N_CTX)
    queries = query_rows[order].reshape(TOKENS, KV_HEADS, group_size, HEAD_DIM)
    grads = out_grad[order].reshape(TOKENS, KV_HEADS, group_size, HEAD_DIM)
    pad_rows = jnp.zeros((DOCMAX, KV_HEADS, HEAD_DIM), key_rows.dtype)
    key_pad = jnp.concatenate([pad_rows, key_rows[order].reshape(TOKENS, KV_HEADS, HEAD_DIM)], axis=0)
    value_pad = jnp.concatenate([pad_rows, value_rows[order].reshape(TOKENS, KV_HEADS, HEAD_DIM)], axis=0)
    positions = jnp.arange(TOKENS, dtype=jnp.int32)
    doc_ids = documents(positions, doc_lengths)
    key_pos = jnp.concatenate([jnp.zeros((DOCMAX,), jnp.int32), positions])
    key_doc = jnp.concatenate([jnp.full((DOCMAX,), -1, dtype=jnp.int32), doc_ids])

    def block(carried, block_index):
        key_full, value_full = carried
        row_start = (block_index * block_len).astype(jnp.int32)
        query_block = lax.dynamic_slice_in_dim(queries, row_start, block_len, 0).astype(jnp.float32)
        grad_block = lax.dynamic_slice_in_dim(grads, row_start, block_len, 0).astype(jnp.float32)
        query_pos = lax.dynamic_slice_in_dim(positions, row_start, block_len, 0)
        query_doc = lax.dynamic_slice_in_dim(doc_ids, row_start, block_len, 0)
        key_block = lax.dynamic_slice_in_dim(key_pad, row_start, span_len, 0).astype(jnp.float32)
        value_block = lax.dynamic_slice_in_dim(value_pad, row_start, span_len, 0).astype(jnp.float32)
        span_pos = lax.dynamic_slice_in_dim(key_pos, row_start, span_len, 0)
        span_doc = lax.dynamic_slice_in_dim(key_doc, row_start, span_len, 0)
        allowed = (span_doc[None, :] == query_doc[:, None]) & (span_pos[None, :] <= query_pos[:, None])
        allowed = allowed[:, None, None, :]
        scores = jnp.einsum("qgjd,kgd->qgjk", query_block, key_block) * scaling
        masked = jnp.where(allowed, scores, -jnp.inf)
        row_top = jnp.max(masked, axis=-1)
        log_total = row_top + jnp.log(jnp.sum(jnp.exp(masked - row_top[..., None]), axis=-1))
        weights = jnp.exp(jnp.where(allowed, scores - log_total[..., None], -jnp.inf))
        weights_low = settle(weights)
        attended_block = jnp.einsum("qgjk,kgd->qgjd", weights_low, value_block).astype(jnp.bfloat16)
        row_delta = jnp.sum(grad_block * attended_block.astype(jnp.float32), axis=-1)
        weight_grad = jnp.einsum("qgjd,kgd->qgjk", grad_block, value_block)
        score_grad = settle(weights * (weight_grad - row_delta[..., None]))
        query_block_grad = (jnp.einsum("qgjk,kgd->qgjd", score_grad, key_block) * scaling).astype(jnp.bfloat16)
        key_part = jnp.einsum("qgjk,qgjd->kgd", score_grad, query_block) * scaling
        value_part = jnp.einsum("qgjk,qgjd->kgd", weights_low, grad_block)
        previous = lax.dynamic_slice_in_dim(key_full, row_start, span_len, 0)
        key_full = lax.dynamic_update_slice_in_dim(key_full, previous + key_part, row_start, 0)
        previous = lax.dynamic_slice_in_dim(value_full, row_start, span_len, 0)
        value_full = lax.dynamic_update_slice_in_dim(value_full, previous + value_part, row_start, 0)
        return (key_full, value_full), (attended_block, query_block_grad)

    start_state = (jnp.zeros((DOCMAX + TOKENS, KV_HEADS, HEAD_DIM), jnp.float32),
                   jnp.zeros((DOCMAX + TOKENS, KV_HEADS, HEAD_DIM), jnp.float32))
    (key_full, value_full), (attended_pos, query_pos_grad) = lax.scan(
        block, start_state, jnp.arange(TOKENS // block_len, dtype=jnp.int32))
    attended = attended_pos.reshape(TOKENS, HEADS * HEAD_DIM)[inverse]
    query_grad = query_pos_grad.reshape(TOKENS, HEADS * HEAD_DIM)[inverse]
    key_grad = key_full[DOCMAX:].reshape(TOKENS, KV_HEADS * HEAD_DIM)[inverse].astype(jnp.bfloat16)
    value_grad = value_full[DOCMAX:].reshape(TOKENS, KV_HEADS * HEAD_DIM)[inverse].astype(jnp.bfloat16)
    return (attended, query_grad, key_grad, value_grad)
```

```python
import math

import jax
import jax.numpy as jnp
from jax import lax
from jax.experimental import pallas as pl
from jax.experimental.pallas import tpu as pltpu
from jax.sharding import PartitionSpec as P

HEAD_DIM = 128
DOC_STRETCHES = 8
MASKED = -1e30


def exchanges(ctx_count, reach):
    sets = []
    for offset in range(1, reach + 1):
        for colour in range(2):
            firsts = [b for b in range(ctx_count - offset) if (b // offset) % 2 == colour]
            if firsts:
                full = any(2 * b >= 2 * ctx_count - 1 - reach - offset for b in firsts)
                sets.append((offset, colour, full, tuple(firsts)))
    return sets


def swap(value, exchange, ctx_count, head_count):
    offset, _, _, firsts = exchange
    partner = {b: b + offset for b in firsts}
    partner.update({b + offset: b for b in firsts})
    pairs = []
    for b in range(ctx_count):
        for h in range(head_count):
            if b in partner:
                pairs.append((b * head_count + h, partner[b] * head_count + h))
            else:
                pairs.append((b * head_count + h, b * head_count + (h + 1) % head_count))
    return lax.ppermute(value, ("ctx", "head"), pairs)


def fold_offsets(slot):
    return range(-(slot - 1), slot, 2)


def pack_kernel(sets, k_ref, v_ref, *out_refs):
    me = lax.axis_index("ctx")
    length = k_ref.shape[0] // 2
    width = k_ref.shape[1]
    for (offset, colour, full, _), out in zip(sets, out_refs):
        if full:
            out[:, :width] = k_ref[...]
            out[:, width:] = v_ref[...]
        else:
            first = (me // offset) % 2 == colour
            start = pl.multiple_of(jnp.where(first, 0, length), length)
            out[:, :width] = k_ref[pl.ds(start, length), :]
            out[:, width:] = v_ref[pl.ds(start, length), :]


def main_kernel(sets, ctx_count, reach, docs_ref, q_ref, g_ref, k_ref, v_ref, *refs):
    count = len(sets)
    recs = {(s[0], s[1]): (r, s[2]) for s, r in zip(sets, refs[:count])}
    att_ref, dq_ref, own_ref = refs[count : count + 3]
    sends = {(s[0], s[1]): (r, s[2]) for s, r in zip(sets, refs[count + 3 : 2 * count + 3])}
    kv_win, bias, pb, dsb, acc, extra = refs[2 * count + 3 :]
    me = lax.axis_index("ctx")
    length = k_ref.shape[0] // 2
    width = HEAD_DIM
    heads = q_ref.shape[1] // width
    span = (reach + 1) * length
    scaling = width ** (-0.5)
    log_scale = scaling * math.log2(math.e)

    def low_part(key):
        ref, full = recs[key]
        return ref[:length, :] if full else ref[...]

    def up_part(key):
        ref, full = recs[key]
        return ref[length:, :] if full else ref[...]

    def choose(pred, a, b):
        return jnp.where(pred, a, b)

    def pick(part, offset, colour_pred):
        have = [c for c in range(2) if (offset, c) in recs]
        if len(have) == 1:
            return part((offset, have[0]))
        return choose(colour_pred, part((offset, 1)), part((offset, 0)))

    def own(half):
        rows = slice(half * length, (half + 1) * length)
        return jnp.concatenate([k_ref[rows, :], v_ref[rows, :]], axis=1)

    lows = [own(0)]
    highs = [own(1)]
    for slot in range(1, reach + 1):
        odd = (me // slot) % 2 == 1
        lows.append(pick(low_part, slot, jnp.logical_not(odd)))
        value = pick(up_part, slot, odd)
        highs.append(value)
    for slot in range(1, reach + 1):
        folded = me + slot >= ctx_count
        value = highs[slot]
        for offset in fold_offsets(slot):
            here = folded & (2 * ctx_count - 1 - 2 * me - slot == offset)
            if offset <= 0:
                value = choose(here, lows[-offset], value)
            else:
                for colour in range(2):
                    if recs.get((offset, colour), (None, False))[1]:
                        mine = here & ((me // offset) % 2 == colour)
                        value = choose(mine, low_part((offset, colour)), value)
        highs[slot] = value
    for slot in range(reach + 1):
        rows = slice(slot * length, (slot + 1) * length)
        kv_win[0, rows, :] = lows[slot]
        kv_win[1, rows, :] = highs[slot]

    row = lax.broadcasted_iota(jnp.int32, (span, length), 0)
    col = lax.broadcasted_iota(jnp.int32, (1, length), 1)
    group = 2 if heads % 2 == 0 else 1
    for s in range(2):
        stretch = me if s == 0 else 2 * ctx_count - 1 - me
        q_pos = stretch * length + col
        start = jnp.int32(0)
        doc_start = jnp.zeros((1, length), jnp.int32)
        for i in range(docs_ref.shape[0]):
            doc_start = jnp.where(q_pos >= start, start, doc_start)
            start = start + docs_ref[i]
        k_pos = row + (stretch - 2 * (row // length)) * length
        allowed = (k_pos >= doc_start) & (k_pos <= q_pos)
        bias[...] = jnp.where(allowed, 0.0, MASKED)
        k_win = kv_win[s, :, :width]
        v_win = kv_win[s, :, width:]
        k_turn = k_win.T
        v_turn = v_win.T
        rows = slice(s * length, (s + 1) * length)
        for h in range(0, heads, group):
            cols = [slice((h + i) * width, (h + i + 1) * width) for i in range(group)]
            lanes = slice(h * length, (h + group) * length)
            q_pair = jnp.concatenate([q_ref[rows, c] for c in cols], axis=0)
            g_pair = jnp.concatenate([g_ref[rows, c] for c in cols], axis=0)
            contract_last = (((1,), (1,)), ((), ()))
            raw = lax.dot_general(k_win, q_pair, contract_last, preferred_element_type=jnp.float32)
            d_p = lax.dot_general(v_win, g_pair, contract_last, preferred_element_type=jnp.float32)
            shift = bias[...]
            raw = raw + jnp.concatenate([shift] * group, axis=1)
            top = jnp.max(raw, axis=0, keepdims=True)
            weight = jnp.exp2((raw - top) * log_scale)
            total = jnp.sum(weight, axis=0, keepdims=True)
            weight = weight * (1.0 / total)
            delta = jnp.sum(weight * d_p, axis=0, keepdims=True)
            low = weight.astype(jnp.bfloat16)
            d_s = (weight * (d_p - delta)).astype(jnp.bfloat16)
            pb[s, :, lanes] = low
            dsb[s, :, lanes] = d_s
            out_t = jnp.dot(v_turn, low, preferred_element_type=jnp.float32).astype(jnp.bfloat16)
            dq_t = jnp.dot(k_turn, d_s, preferred_element_type=jnp.float32) * scaling
            dq_t = dq_t.astype(jnp.bfloat16)
            for i in range(group):
                part = slice(i * length, (i + 1) * length)
                att_ref[rows, cols[i]] = out_t[:, part].T
                dq_ref[rows, cols[i]] = dq_t[:, part].T
        q_all = jnp.concatenate(
            [q_ref[rows, h * width : (h + 1) * width] for h in range(heads)], axis=0
        )
        g_all = jnp.concatenate(
            [g_ref[rows, h * width : (h + 1) * width] for h in range(heads)], axis=0
        )
        d_k = jnp.dot(dsb[s], q_all, preferred_element_type=jnp.float32) * scaling
        d_v = jnp.dot(pb[s], g_all, preferred_element_type=jnp.float32)
        acc[s, :, :width] = d_k
        acc[s, :, width:] = d_v

    def slot_rows(slot):
        return slice(slot * length, (slot + 1) * length)

    extra[...] = jnp.zeros(extra.shape, jnp.float32)
    for slot in range(1, reach + 1):
        for offset in fold_offsets(slot):

            @pl.when((me + slot >= ctx_count) & (2 * ctx_count - 1 - 2 * me - slot == offset))
            def _():
                part = acc[1, slot_rows(slot), :]
                if offset <= 0:
                    acc[0, slot_rows(-offset), :] = acc[0, slot_rows(-offset), :] + part
                else:
                    extra[slot_rows(offset - 1), :] = part

    own_ref[:length, :] = acc[0, :length, :]
    own_ref[length:, :] = acc[1, :length, :]
    for (offset, colour), (ref, full) in sends.items():
        first = (me // offset) % 2 == colour
        to_low = acc[0, slot_rows(offset), :]
        to_up = acc[1, slot_rows(offset), :]
        if full:
            more = extra[slot_rows(offset - 1), :]
            ref[:length, :] = jnp.where(first, more, to_low).astype(jnp.bfloat16)
            ref[length:, :] = jnp.where(first, to_up, 0.0).astype(jnp.bfloat16)
        else:
            ref[...] = jnp.where(first, to_up, to_low).astype(jnp.bfloat16)


def sum_kernel(sets, ctx_count, own_ref, *refs):
    dk_ref, dv_ref = refs[len(sets) :]
    me = lax.axis_index("ctx")
    length = own_ref.shape[0] // 2
    width = dk_ref.shape[1]
    low = own_ref[:length, :]
    up = own_ref[length:, :]
    for (offset, colour, full, _), ref in zip(sets, refs):
        first = (me // offset) % 2 == colour
        as_first = first & (me + offset < ctx_count)
        as_second = jnp.logical_not(first) & (me >= offset)
        if full:
            low = low + jnp.where(as_first | as_second, ref[:length, :].astype(jnp.float32), 0.0)
            up = up + jnp.where(as_second, ref[length:, :].astype(jnp.float32), 0.0)
        else:
            part = ref[...].astype(jnp.float32)
            low = low + jnp.where(as_first, part, 0.0)
            up = up + jnp.where(as_second, part, 0.0)
    dk_ref[:length, :] = low[:, :width].astype(jnp.bfloat16)
    dk_ref[length:, :] = up[:, :width].astype(jnp.bfloat16)
    dv_ref[:length, :] = low[:, width:].astype(jnp.bfloat16)
    dv_ref[length:, :] = up[:, width:].astype(jnp.bfloat16)


def in_vmem(amount):
    return [pl.BlockSpec(memory_space=pltpu.VMEM)] * amount


def shards(query_rows, key_rows, value_rows, out_grad, doc_lengths):
    ctx_count = lax.axis_size("ctx")
    head_count = lax.axis_size("head")
    tok_dev = query_rows.shape[0]
    length = tok_dev // 2
    width = key_rows.shape[1]
    reach = min(DOC_STRETCHES, ctx_count // 4)
    span = (reach + 1) * length
    heads = query_rows.shape[1] // width
    sets = exchanges(ctx_count, reach)
    payloads = [
        jax.ShapeDtypeStruct((2 * length if s[2] else length, 2 * width), jnp.bfloat16)
        for s in sets
    ]
    count = len(sets)

    packed = pl.pallas_call(
        lambda *refs: pack_kernel(sets, *refs),
        out_shape=payloads,
        in_specs=in_vmem(2),
        out_specs=in_vmem(count),
        name="pack",
    )(key_rows, value_rows)
    received = [swap(p, s, ctx_count, head_count) for p, s in zip(packed, sets)]

    results = pl.pallas_call(
        lambda *refs: main_kernel(sets, ctx_count, reach, *refs),
        out_shape=[
            jax.ShapeDtypeStruct(query_rows.shape, jnp.bfloat16),
            jax.ShapeDtypeStruct(query_rows.shape, jnp.bfloat16),
            jax.ShapeDtypeStruct((tok_dev, 2 * width), jnp.float32),
        ]
        + payloads,
        in_specs=[pl.BlockSpec(memory_space=pltpu.SMEM)] + in_vmem(4 + count),
        out_specs=in_vmem(3 + count),
        scratch_shapes=[
            pltpu.VMEM((2, span, 2 * width), jnp.bfloat16),
            pltpu.VMEM((span, length), jnp.float32),
            pltpu.VMEM((2, span, heads * length), jnp.bfloat16),
            pltpu.VMEM((2, span, heads * length), jnp.bfloat16),
            pltpu.VMEM((2, span, 2 * width), jnp.float32),
            pltpu.VMEM((reach * length, 2 * width), jnp.float32),
        ],
        name="attend",
    )(doc_lengths, query_rows, out_grad, key_rows, value_rows, *received)
    attended, query_grad, own = results[:3]
    returned = [swap(p, s, ctx_count, head_count) for p, s in zip(results[3:], sets)]

    key_grad, value_grad = pl.pallas_call(
        lambda *refs: sum_kernel(sets, ctx_count, *refs),
        out_shape=[jax.ShapeDtypeStruct(key_rows.shape, jnp.bfloat16)] * 2,
        in_specs=in_vmem(1 + count),
        out_specs=in_vmem(2),
        name="total",
    )(own, *returned)
    return (attended, query_grad, key_grad, value_grad)


def solution(mesh):
    placed = (
        P(("groups", "ctx"), "head"),
        P(("groups", "ctx"), "head"),
        P(("groups", "ctx"), "head"),
        P(("groups", "ctx"), "head"),
        P("groups"),
    )
    return jax.shard_map(
        shards,
        mesh=mesh,
        in_specs=placed,
        out_specs=(P(("groups", "ctx"), "head"),) * 4,
        check_vma=False,
    )
```

```python
import math

import jax
import jax.numpy as jnp
from jax import lax
from jax.experimental import pallas as pl
from jax.experimental.pallas import tpu as pltpu
from jax.sharding import PartitionSpec as P

HEAD_DIM = 128
DOC_STRETCHES = 8
MASKED = -1e30
VMEM_LIMIT = 24 << 20


def exchanges(ctx_count, reach):
    sets = []
    for offset in range(1, reach + 1):
        for colour in range(2):
            firsts = [b for b in range(ctx_count - offset) if (b // offset) % 2 == colour]
            if firsts:
                full = any(2 * b >= 2 * ctx_count - 1 - reach - offset for b in firsts)
                sets.append((offset, colour, full, tuple(firsts)))
    return sets


def swap(value, exchange, ctx_count, head_count):
    offset, _, _, firsts = exchange
    partner = {b: b + offset for b in firsts}
    partner.update({b + offset: b for b in firsts})
    pairs = []
    for b in range(ctx_count):
        for h in range(head_count):
            if b in partner:
                pairs.append((b * head_count + h, partner[b] * head_count + h))
            else:
                pairs.append((b * head_count + h, b * head_count + (h + 1) % head_count))
    return lax.ppermute(value, ("ctx", "head"), pairs)


def fold_offsets(slot):
    return range(-(slot - 1), slot, 2)


def pack_kernel(sets, k_hbm, v_hbm, mine, *refs):
    halves = [s for s in sets if not s[2]]
    outs, sems = refs[: len(halves)], refs[len(halves)]
    me = lax.axis_index("ctx")
    length = k_hbm.shape[0] // 2
    width = k_hbm.shape[1]
    copies = [
        pltpu.make_async_copy(k_hbm, mine.at[:, :width], sems.at[0]),
        pltpu.make_async_copy(v_hbm, mine.at[:, width:], sems.at[1]),
    ]
    for i, ((offset, colour, _, _), out) in enumerate(zip(halves, outs)):
        first = (me // offset) % 2 == colour
        rows = pl.ds(pl.multiple_of(jnp.where(first, 0, length), length), length)
        copies.append(pltpu.make_async_copy(k_hbm.at[rows, :], out.at[:, :width], sems.at[2 * i + 2]))
        copies.append(pltpu.make_async_copy(v_hbm.at[rows, :], out.at[:, width:], sems.at[2 * i + 3]))
    for copy in copies:
        copy.start()
    for copy in copies:
        copy.wait()


def stage_kernel(ctx_count, docs_ref, q_hbm, g_hbm, q_all, g_all, bias, sems):
    length = q_hbm.shape[0] // 2
    width = q_all.shape[2]
    heads = q_all.shape[1] // length
    copies = []
    for s in range(2):
        for h in range(heads):
            for a, (src, dst) in enumerate(((q_hbm, q_all), (g_hbm, g_all))):
                copies.append(
                    pltpu.make_async_copy(
                        src.at[s * length : (s + 1) * length, h * width : (h + 1) * width],
                        dst.at[s, h * length : (h + 1) * length, :],
                        sems.at[a, s, h],
                    )
                )
    for copy in copies:
        copy.start()
    me = lax.axis_index("ctx")
    merged = bias.shape[1]
    row = lax.broadcasted_iota(jnp.int32, (merged, length), 0)
    col = lax.broadcasted_iota(jnp.int32, (1, length), 1)
    for s in range(2):
        stretch = me if s == 0 else 2 * ctx_count - 1 - me
        q_pos = stretch * length + col
        start = jnp.int32(0)
        doc_start = jnp.zeros((1, length), jnp.int32)
        for i in range(docs_ref.shape[0]):
            doc_start = jnp.where(q_pos >= start, start, doc_start)
            start = start + docs_ref[i]
        k_pos = row + (stretch - 2 * (row // length)) * length
        k_pos = jnp.where(k_pos > q_pos, k_pos - merged, k_pos)
        bias[s] = jnp.where(k_pos >= doc_start, 0.0, MASKED)
    for copy in copies:
        copy.wait()


def score_kernel(sets, ctx_count, reach, bias, q_all, g_all, mine, *refs):
    halves = [s for s in sets if not s[2]]
    fulls = [s for s in sets if s[2]]
    order = fulls + halves
    count = len(order)
    recs = {(s[0], s[1]): (r, s[2]) for s, r in zip(order, refs[:count])}
    pb, dsb, kv_win, own_ref = refs[count : count + 4]
    sends = {(s[0], s[1]): (r, s[2]) for s, r in zip(order, refs[count + 4 : 2 * count + 4])}
    acc, extra = refs[2 * count + 4 :]
    me = lax.axis_index("ctx")
    length = mine.shape[0] // 2
    width = HEAD_DIM
    heads = q_all.shape[1] // length
    merged = reach * length
    scaling = width ** (-0.5)
    log_scale = scaling * math.log2(math.e)

    def low_part(key):
        ref, full = recs[key]
        return ref[:length, :] if full else ref[...]

    def up_part(key):
        ref, full = recs[key]
        return ref[length:, :] if full else ref[...]

    def pick(part, offset, colour_pred):
        have = [c for c in range(2) if (offset, c) in recs]
        if len(have) == 1:
            return part((offset, have[0]))
        return jnp.where(colour_pred, part((offset, 1)), part((offset, 0)))

    lows = [mine[:length, :]]
    highs = [mine[length:, :]]
    for slot in range(1, reach + 1):
        odd = (me // slot) % 2 == 1
        lows.append(pick(low_part, slot, jnp.logical_not(odd)))
        highs.append(pick(up_part, slot, odd))
    for slot in range(1, reach + 1):
        folded = me + slot >= ctx_count
        value = highs[slot]
        for offset in fold_offsets(slot):
            here = folded & (2 * ctx_count - 1 - 2 * me - slot == offset)
            if offset <= 0:
                value = jnp.where(here, lows[-offset], value)
            else:
                for colour in range(2):
                    if recs.get((offset, colour), (None, False))[1]:
                        where = here & ((me // offset) % 2 == colour)
                        value = jnp.where(where, low_part((offset, colour)), value)
        highs[slot] = value
    for slot in range(reach + 1):
        rows = slice(slot * length, (slot + 1) * length)
        kv_win[0, rows, :] = lows[slot]
        kv_win[1, rows, :] = highs[slot]

    tri_row = lax.broadcasted_iota(jnp.int32, (length, length), 0)
    near = tri_row <= lax.broadcasted_iota(jnp.int32, (length, length), 1)
    near_low = jnp.where(near, 1.0, 0.0).astype(jnp.bfloat16)

    def fold(value):
        return jnp.where(near, value[:length, :], value[merged:, :])

    def products(s, h):
        lanes = slice(h * length, (h + 1) * length)
        contract_last = (((1,), (1,)), ((), ()))
        raw = lax.dot_general(
            kv_win[s, :, :width], q_all[s, lanes, :], contract_last, preferred_element_type=jnp.float32
        )
        d_p = lax.dot_general(
            kv_win[s, :, width:], g_all[s, lanes, :], contract_last, preferred_element_type=jnp.float32
        )
        return raw, d_p

    def soften(s, h, raw, d_p):
        lanes = slice(h * length, (h + 1) * length)
        raw = jnp.concatenate([fold(raw), raw[length:merged, :]], axis=0) + bias[s]
        d_p = jnp.concatenate([fold(d_p), d_p[length:merged, :]], axis=0)
        top = jnp.max(raw, axis=0, keepdims=True)
        weight = jnp.exp2((raw - top) * log_scale)
        total = jnp.sum(weight, axis=0, keepdims=True)
        inverse = 1.0 / total
        delta = jnp.sum(weight * d_p, axis=0, keepdims=True) * inverse
        weight = weight * inverse
        low = weight.astype(jnp.bfloat16)
        d_s = (weight * (d_p - delta)).astype(jnp.bfloat16)
        for ref, value in ((pb, low), (dsb, d_s)):
            here = value[:length, :] * near_low
            ref[s, :length, lanes] = here
            ref[s, length:merged, lanes] = value[length:, :]
            ref[s, merged:, lanes] = value[:length, :] - here

    def gradients(s):
        acc[s, :, :width] = jnp.dot(dsb[s], q_all[s], preferred_element_type=jnp.float32) * scaling
        acc[s, :, width:] = jnp.dot(pb[s], g_all[s], preferred_element_type=jnp.float32)

    items = [(s, h) for s in range(2) for h in range(heads)]
    ready = products(*items[0])
    for i, item in enumerate(items):
        following = products(*items[i + 1]) if i + 1 < len(items) else None
        soften(*item, *ready)
        ready = following
        if item[1] == heads - 1:
            gradients(item[0])

    def slot_rows(slot):
        return slice(slot * length, (slot + 1) * length)

    extra[...] = jnp.zeros(extra.shape, jnp.float32)
    for slot in range(1, reach + 1):
        for offset in fold_offsets(slot):

            @pl.when((me + slot >= ctx_count) & (2 * ctx_count - 1 - 2 * me - slot == offset))
            def _():
                part = acc[1, slot_rows(slot), :]
                if offset <= 0:
                    acc[0, slot_rows(-offset), :] = acc[0, slot_rows(-offset), :] + part
                else:
                    extra[slot_rows(offset - 1), :] = part

    own_ref[:length, :] = acc[0, :length, :]
    own_ref[length:, :] = acc[1, :length, :]
    for (offset, colour), (ref, full) in sends.items():
        first = (me // offset) % 2 == colour
        to_low = acc[0, slot_rows(offset), :]
        to_up = acc[1, slot_rows(offset), :]
        if full:
            more = extra[slot_rows(offset - 1), :]
            ref[:length, :] = jnp.where(first, more, to_low).astype(jnp.bfloat16)
            ref[length:, :] = jnp.where(first, to_up, 0.0).astype(jnp.bfloat16)
        else:
            ref[...] = jnp.where(first, to_up, to_low).astype(jnp.bfloat16)


def output_kernel(pb, dsb, kv_win, att_hbm, dq_hbm, att, dq, sems):
    length = att.shape[0] // 2
    width = HEAD_DIM
    heads = att.shape[1] // width
    scaling = width ** (-0.5)
    group = 2 if heads % 2 == 0 else 1
    copies = []
    for s in range(2):
        rows = slice(s * length, (s + 1) * length)
        k_turn = kv_win[s, :, :width].T
        v_turn = kv_win[s, :, width:].T
        for h in range(0, heads, group):
            lanes = slice(h * length, (h + group) * length)
            out_t = jnp.dot(v_turn, pb[s, :, lanes], preferred_element_type=jnp.float32)
            dq_t = jnp.dot(k_turn, dsb[s, :, lanes], preferred_element_type=jnp.float32) * scaling
            out_t = out_t.astype(jnp.bfloat16)
            dq_t = dq_t.astype(jnp.bfloat16)
            for i in range(group):
                part = slice(i * length, (i + 1) * length)
                cols = slice((h + i) * width, (h + i + 1) * width)
                att[rows, cols] = out_t[:, part].T
                dq[rows, cols] = dq_t[:, part].T
        for a, (src, dst) in enumerate(((att, att_hbm), (dq, dq_hbm))):
            copy = pltpu.make_async_copy(src.at[rows, :], dst.at[rows, :], sems.at[s, a])
            copy.start()
            copies.append(copy)
    for copy in copies:
        copy.wait()


def sum_kernel(sets, ctx_count, own_ref, *refs):
    dk_ref, dv_ref = refs[len(sets) :]
    me = lax.axis_index("ctx")
    length = own_ref.shape[0] // 2
    width = dk_ref.shape[1]
    low = own_ref[:length, :]
    up = own_ref[length:, :]
    for (offset, colour, full, _), ref in zip(sets, refs):
        first = (me // offset) % 2 == colour
        as_first = first & (me + offset < ctx_count)
        as_second = jnp.logical_not(first) & (me >= offset)
        if full:
            low = low + jnp.where(as_first | as_second, ref[:length, :].astype(jnp.float32), 0.0)
            up = up + jnp.where(as_second, ref[length:, :].astype(jnp.float32), 0.0)
        else:
            part = ref[...].astype(jnp.float32)
            low = low + jnp.where(as_first, part, 0.0)
            up = up + jnp.where(as_second, part, 0.0)
    dk_ref[:length, :] = low[:, :width].astype(jnp.bfloat16)
    dk_ref[length:, :] = up[:, :width].astype(jnp.bfloat16)
    dv_ref[:length, :] = low[:, width:].astype(jnp.bfloat16)
    dv_ref[length:, :] = up[:, width:].astype(jnp.bfloat16)


def in_vmem(amount):
    return [pl.BlockSpec(memory_space=pltpu.VMEM)] * amount


def in_place(amount):
    return [pl.BlockSpec(memory_space=pl.ANY)] * amount


def on_chip(values):
    return [pltpu.with_memory_space_constraint(v, pltpu.VMEM) for v in values]


def off_chip(values):
    return [pltpu.with_memory_space_constraint(v, pltpu.HBM) for v in values]


def shards(query_rows, key_rows, value_rows, out_grad, doc_lengths):
    ctx_count = lax.axis_size("ctx")
    head_count = lax.axis_size("head")
    tok_dev = query_rows.shape[0]
    length = tok_dev // 2
    width = key_rows.shape[1]
    reach = min(DOC_STRETCHES, ctx_count // 4)
    span = (reach + 1) * length
    heads = query_rows.shape[1] // width
    sets = exchanges(ctx_count, reach)
    sets = [s for s in sets if s[2]] + [s for s in sets if not s[2]]
    fulls = sum(s[2] for s in sets)
    count = len(sets)
    payloads = [
        pltpu.VMEM((2 * length if s[2] else length, 2 * width), jnp.bfloat16) for s in sets
    ]
    mine, *halves = pl.pallas_call(
        lambda *refs: pack_kernel(sets, *refs),
        out_shape=[pltpu.VMEM((tok_dev, 2 * width), jnp.bfloat16)] + payloads[fulls:],
        in_specs=in_place(2),
        out_specs=in_vmem(1 + count - fulls),
        scratch_shapes=[pltpu.SemaphoreType.DMA((2 + 2 * (count - fulls),))],
        compiler_params=pltpu.CompilerParams(vmem_limit_bytes=VMEM_LIMIT),
        name="pack",
    )(*off_chip([key_rows, value_rows]))
    packed = [mine] * fulls + halves
    received = [swap(p, s, ctx_count, head_count) for p, s in zip(packed, sets)]

    stack = pltpu.VMEM((2, heads * length, width), jnp.bfloat16)
    q_all, g_all, bias = pl.pallas_call(
        lambda *refs: stage_kernel(ctx_count, *refs),
        out_shape=[stack, stack, pltpu.VMEM((2, reach * length, length), jnp.float32)],
        in_specs=[pl.BlockSpec(memory_space=pltpu.SMEM)] + in_place(2),
        out_specs=in_vmem(3),
        scratch_shapes=[pltpu.SemaphoreType.DMA((2, 2, heads))],
        compiler_params=pltpu.CompilerParams(vmem_limit_bytes=VMEM_LIMIT),
        name="stage",
    )(doc_lengths, *off_chip([query_rows, out_grad]))

    low_weights = pltpu.VMEM((2, span, heads * length), jnp.bfloat16)
    pb, dsb, kv_win, own, *partials = pl.pallas_call(
        lambda *refs: score_kernel(sets, ctx_count, reach, *refs),
        out_shape=[
            low_weights,
            low_weights,
            pltpu.VMEM((2, span, 2 * width), jnp.bfloat16),
            pltpu.VMEM((tok_dev, 2 * width), jnp.float32),
        ]
        + payloads,
        in_specs=in_vmem(4 + count),
        out_specs=in_vmem(4 + count),
        scratch_shapes=[
            pltpu.VMEM((2, span, 2 * width), jnp.float32),
            pltpu.VMEM((reach * length, 2 * width), jnp.float32),
        ],
        compiler_params=pltpu.CompilerParams(vmem_limit_bytes=VMEM_LIMIT),
        name="score",
    )(*on_chip([bias, q_all, g_all, mine, *received]))
    returned = [swap(p, s, ctx_count, head_count) for p, s in zip(partials, sets)]

    attended, query_grad = pl.pallas_call(
        output_kernel,
        out_shape=[jax.ShapeDtypeStruct(query_rows.shape, jnp.bfloat16)] * 2,
        in_specs=in_vmem(3),
        out_specs=in_place(2),
        scratch_shapes=[
            pltpu.VMEM(query_rows.shape, jnp.bfloat16),
            pltpu.VMEM(query_rows.shape, jnp.bfloat16),
            pltpu.SemaphoreType.DMA((2, 2)),
        ],
        compiler_params=pltpu.CompilerParams(vmem_limit_bytes=VMEM_LIMIT),
        name="output",
    )(*on_chip([pb, dsb, kv_win]))

    key_grad, value_grad = pl.pallas_call(
        lambda *refs: sum_kernel(sets, ctx_count, *refs),
        out_shape=[jax.ShapeDtypeStruct(key_rows.shape, jnp.bfloat16)] * 2,
        in_specs=in_vmem(1 + count),
        out_specs=in_vmem(2),
        compiler_params=pltpu.CompilerParams(vmem_limit_bytes=VMEM_LIMIT),
        name="total",
    )(*on_chip([own, *returned]))
    return (attended, query_grad, key_grad, value_grad)


def solution(mesh):
    placed = (
        P(("groups", "ctx"), "head"),
        P(("groups", "ctx"), "head"),
        P(("groups", "ctx"), "head"),
        P(("groups", "ctx"), "head"),
        P("groups"),
    )
    return jax.shard_map(
        shards,
        mesh=mesh,
        in_specs=placed,
        out_specs=(P(("groups", "ctx"), "head"),) * 4,
        check_vma=False,
    )
```

```python
import math

import jax
import jax.numpy as jnp
from jax import lax
from jax.experimental import pallas as pl
from jax.experimental.pallas import tpu as pltpu
from jax.sharding import PartitionSpec as P

HEAD_DIM = 128
DOC_STRETCHES = 8
MASKED = -1e30
VMEM_LIMIT = 24 << 20
CHUNK = 4


def exchanges(ctx_count, reach):
    sets = []
    for offset in range(1, reach + 1):
        for colour in range(2):
            firsts = [b for b in range(ctx_count - offset) if (b // offset) % 2 == colour]
            if firsts:
                sets.append(dict(offset=offset, colour=colour, full=False, firsts=firsts, folds=[]))
    while not place_folds(sets, ctx_count, reach):
        pass
    return sorted(sets, key=lambda entry: not entry["full"])


def place_folds(sets, ctx_count, reach):
    for entry in sets:
        entry["folds"] = []
    for entry in sets:
        offset = entry["offset"]
        for b in entry["firsts"]:
            if entry["full"] or 2 * b < 2 * ctx_count - 1 - reach - offset:
                continue
            for other in sets:
                busy = [x for f in other["firsts"] for x in (f, f + other["offset"])]
                busy += [x for pair in other["folds"] for x in pair]
                sends_low = ((b + offset) // other["offset"]) % 2 == other["colour"]
                if b not in busy and b + offset not in busy and sends_low and not other["full"]:
                    other["folds"].append((b, b + offset))
                    break
            else:
                entry["full"] = True
                return False
    return True


def key_of(entry):
    return entry["offset"], entry["colour"]


def swap(value, exchange, ctx_count, head_count, phase):
    partner = {}
    pairs = [(b, b + exchange["offset"]) for b in exchange["firsts"]] + exchange["folds"]
    for a, b in pairs:
        partner[a], partner[b] = b, a
    pairs = []
    for b in range(ctx_count):
        for h in range(head_count):
            if b in partner:
                pairs.append((b * head_count + h, partner[b] * head_count + h))
            else:
                pairs.append((b * head_count + h, b * head_count + (h + 1) % head_count))
    with jax.named_scope(f"{phase}_{exchange['offset']}_{exchange['colour']}"):
        return lax.ppermute(value, ("ctx", "head"), pairs)


def fold_offsets(slot):
    return range(-(slot - 1), slot, 2)


def pack_kernel(sets, k_hbm, v_hbm, mine, *refs):
    halves = [s for s in sets if not s["full"]]
    outs, sems = refs[: len(halves)], refs[len(halves)]
    me = lax.axis_index("ctx")
    length = k_hbm.shape[0] // 2
    width = k_hbm.shape[1]
    copies = [
        pltpu.make_async_copy(k_hbm, mine.at[:, :width], sems.at[0]),
        pltpu.make_async_copy(v_hbm, mine.at[:, width:], sems.at[1]),
    ]
    for i, (entry, out) in enumerate(zip(halves, outs)):
        first = (me // entry["offset"]) % 2 == entry["colour"]
        rows = pl.ds(pl.multiple_of(jnp.where(first, 0, length), length), length)
        copies.append(pltpu.make_async_copy(k_hbm.at[rows, :], out.at[:, :width], sems.at[2 * i + 2]))
        copies.append(pltpu.make_async_copy(v_hbm.at[rows, :], out.at[:, width:], sems.at[2 * i + 3]))
    for copy in copies:
        copy.start()
    for copy in copies:
        copy.wait()


def stage_kernel(ctx_count, docs_hbm, q_hbm, g_hbm, q_all, g_all, bias, docs_ref, sems):
    length = q_hbm.shape[0] // 2
    heads, _, width = q_all.shape
    lengths = pltpu.make_async_copy(docs_hbm, docs_ref, sems.at[2, 0])
    lengths.start()
    copies = []
    for h in range(heads):
        cols = slice(h * width, (h + 1) * width)
        for a, (src, dst) in enumerate(((q_hbm, q_all), (g_hbm, g_all))):
            copies.append(pltpu.make_async_copy(src.at[:, cols], dst.at[h], sems.at[a, h]))
    for copy in copies:
        copy.start()
    lengths.wait()
    me = lax.axis_index("ctx")
    merged = bias.shape[1]
    row = lax.broadcasted_iota(jnp.int32, (merged, length), 0)
    col = lax.broadcasted_iota(jnp.int32, (1, length), 1)
    for s in range(2):
        stretch = me if s == 0 else 2 * ctx_count - 1 - me
        q_pos = stretch * length + col
        start = jnp.int32(0)
        doc_start = jnp.zeros((1, length), jnp.int32)
        for i in range(docs_ref.shape[0]):
            doc_start = jnp.where(q_pos >= start, start, doc_start)
            start = start + docs_ref[i]
        k_pos = row + (stretch - 2 * (row // length)) * length
        k_pos = jnp.where(k_pos > q_pos, k_pos - merged, k_pos)
        bias[s] = jnp.where(k_pos >= doc_start, 0.0, MASKED)
    for copy in copies:
        copy.wait()


def stacked(ref, s, first=0, last=None):
    length = ref.shape[1] // 2
    value = ref[first:last, s * length : (s + 1) * length, :]
    return value.reshape(-1, ref.shape[2])


def beside(ref, s, rows, heads=None):
    heads = range(ref.shape[1]) if heads is None else heads
    return jnp.concatenate([ref[s, h, rows, :] for h in heads], axis=1)


def score_kernel(sets, ctx_count, reach, bias, q_all, g_all, mine, *refs):
    count = len(sets)
    recs = {key_of(s): (r, s["full"]) for s, r in zip(sets, refs[:count])}
    pb, dsb, kv_win, own_ref = refs[count : count + 4]
    send_refs = refs[count + 4 : 2 * count + 4]
    acc, extra = refs[2 * count + 4 :]
    me = lax.axis_index("ctx")
    length = mine.shape[0] // 2
    width = HEAD_DIM
    heads = q_all.shape[0]
    merged = reach * length
    scaling = width ** (-0.5)
    log_scale = scaling * math.log2(math.e)

    def low_part(key):
        ref, full = recs[key]
        return ref[:length, :] if full else ref[...]

    def up_part(key):
        ref, full = recs[key]
        return ref[length:, :] if full else ref[...]

    def pick(part, offset, colour_pred):
        have = [c for c in range(2) if (offset, c) in recs]
        if len(have) == 1:
            return part((offset, have[0]))
        return jnp.where(colour_pred, part((offset, 1)), part((offset, 0)))

    lows = [mine[:length, :]]
    highs = [mine[length:, :]]
    for slot in range(1, reach + 1):
        odd = (me // slot) % 2 == 1
        lows.append(pick(low_part, slot, jnp.logical_not(odd)))
        highs.append(pick(up_part, slot, odd))
    for slot in range(1, reach + 1):
        folded = me + slot >= ctx_count
        value = highs[slot]
        for offset in fold_offsets(slot):
            here = folded & (2 * ctx_count - 1 - 2 * me - slot == offset)
            if offset <= 0:
                value = jnp.where(here, lows[-offset], value)
            else:
                for colour in range(2):
                    if recs.get((offset, colour), (None, False))[1]:
                        where = here & ((me // offset) % 2 == colour)
                        value = jnp.where(where, low_part((offset, colour)), value)
                for entry in sets:
                    for pair in entry["folds"]:
                        if pair[1] - pair[0] == offset:
                            where = here & (me == pair[0])
                            value = jnp.where(where, recs[key_of(entry)][0][...], value)
        highs[slot] = value
    for slot in range(reach + 1):
        rows = slice(slot * length, (slot + 1) * length)
        kv_win[0, rows, :] = lows[slot]
        kv_win[1, rows, :] = highs[slot]

    tri_row = lax.broadcasted_iota(jnp.int32, (length, length), 0)
    near = tri_row <= lax.broadcasted_iota(jnp.int32, (length, length), 1)
    near_low = jnp.where(near, 1.0, 0.0).astype(jnp.bfloat16)

    def fold(value):
        return jnp.where(near, value[:length, :], value[merged:, :])

    def products(s, h):
        contract_last = (((1,), (1,)), ((), ()))
        raw = lax.dot_general(
            kv_win[s, :, :width],
            stacked(q_all, s, h, h + group),
            contract_last,
            preferred_element_type=jnp.float32,
        )
        d_p = lax.dot_general(
            kv_win[s, :, width:],
            stacked(g_all, s, h, h + group),
            contract_last,
            preferred_element_type=jnp.float32,
        )
        return raw, d_p

    def soften(s, h, raw, d_p):
        raw = jnp.concatenate([fold(raw), raw[length:merged, :]], axis=0) + bias[s]
        d_p = jnp.concatenate([fold(d_p), d_p[length:merged, :]], axis=0)
        top = jnp.max(raw, axis=0, keepdims=True)
        weight = jnp.exp2((raw - top) * log_scale)
        total = jnp.sum(weight, axis=0, keepdims=True)
        inverse = 1.0 / total
        delta = jnp.sum(weight * d_p, axis=0, keepdims=True) * inverse
        weight = weight * inverse
        low = weight.astype(jnp.bfloat16)
        d_s = (weight * (d_p - delta)).astype(jnp.bfloat16)
        for ref, value in ((pb, low), (dsb, d_s)):
            here = value[:length, :] * near_low
            ref[s, h, :length, :] = here
            ref[s, h, length:merged, :] = value[length:, :]
            ref[s, h, merged:, :] = value[:length, :] - here

    def gradients(s, first, last):
        part = slice(length, None)
        d_k = jnp.dot(
            beside(dsb, s, part, range(first, last)),
            stacked(q_all, s, first, last),
            preferred_element_type=jnp.float32,
        )
        d_v = jnp.dot(
            beside(pb, s, part, range(first, last)),
            stacked(g_all, s, first, last),
            preferred_element_type=jnp.float32,
        )
        if first > 0:
            d_k = d_k + acc[s, part, :width]
            d_v = d_v + acc[s, part, width:]
        if last == heads:
            d_k = d_k * scaling
        acc[s, part, :width] = d_k
        acc[s, part, width:] = d_v

    chunk = CHUNK if heads % CHUNK == 0 else heads
    group = 2 if heads % 2 == 0 else 1
    items = [(s, h) for s in range(2) for h in range(0, heads, group)]
    ready = products(*items[0])
    for i, (s, h) in enumerate(items):
        following = products(*items[i + 1]) if i + 1 < len(items) else None
        for j in range(group):
            part = slice(j * length, (j + 1) * length)
            soften(s, h + j, ready[0][:, part], ready[1][:, part])
        ready = following
        if (h + group) % chunk == 0:
            gradients(s, h + group - chunk, h + group)

    def slot_rows(slot):
        return slice(slot * length, (slot + 1) * length)

    extra[...] = jnp.zeros(extra.shape, jnp.float32)
    for slot in range(1, reach + 1):
        for offset in fold_offsets(slot):

            @pl.when((me + slot >= ctx_count) & (2 * ctx_count - 1 - 2 * me - slot == offset))
            def _():
                part = acc[1, slot_rows(slot), :]
                if offset < 0:
                    acc[0, slot_rows(-offset), :] = acc[0, slot_rows(-offset), :] + part
                else:
                    extra[slot_rows(offset), :] = part

    own_ref[...] = extra[:length, :]
    for entry, ref in zip(sets, send_refs):
        offset = entry["offset"]
        first = (me // offset) % 2 == entry["colour"]
        to_low = acc[0, slot_rows(offset), :]
        to_up = acc[1, slot_rows(offset), :]
        if entry["full"]:
            more = extra[slot_rows(offset), :]
            ref[:length, :] = jnp.where(first, more, to_low).astype(jnp.bfloat16)
            ref[length:, :] = jnp.where(first, to_up, 0.0).astype(jnp.bfloat16)
        else:
            part = jnp.where(first, to_up, to_low)
            for pair in entry["folds"]:
                part = jnp.where(me == pair[0], extra[slot_rows(pair[1] - pair[0]), :], part)
            ref[...] = part.astype(jnp.bfloat16)


def output_kernel(pb, dsb, kv_win, q_all, g_all, att_hbm, dq_hbm, own_ref, att, dq, sems):
    length = att.shape[0] // 2
    width = HEAD_DIM
    heads = att.shape[1] // width
    scaling = width ** (-0.5)
    group = 2 if heads % 2 == 0 else 1
    copies = []
    for s in range(2):
        rows = slice(s * length, (s + 1) * length)
        k_turn = kv_win[s, :, :width].T
        v_turn = kv_win[s, :, width:].T
        for h in range(0, heads, group):
            pair = range(h, h + group)
            out_t = jnp.dot(v_turn, beside(pb, s, slice(None), pair), preferred_element_type=jnp.float32)
            dq_t = jnp.dot(k_turn, beside(dsb, s, slice(None), pair), preferred_element_type=jnp.float32) * scaling
            out_t = out_t.astype(jnp.bfloat16)
            dq_t = dq_t.astype(jnp.bfloat16)
            for i in range(group):
                part = slice(i * length, (i + 1) * length)
                cols = slice((h + i) * width, (h + i + 1) * width)
                att[rows, cols] = out_t[:, part].T
                dq[rows, cols] = dq_t[:, part].T
        for a, (src, dst) in enumerate(((att, att_hbm), (dq, dq_hbm))):
            copy = pltpu.make_async_copy(src.at[rows, :], dst.at[rows, :], sems.at[s, a])
            copy.start()
            copies.append(copy)
        d_k = jnp.dot(beside(dsb, s, slice(0, length)), stacked(q_all, s), preferred_element_type=jnp.float32)
        d_v = jnp.dot(beside(pb, s, slice(0, length)), stacked(g_all, s), preferred_element_type=jnp.float32)
        own_ref[rows, :width] = d_k * scaling
        own_ref[rows, width:] = d_v
    for copy in copies:
        copy.wait()


def sum_kernel(sets, ctx_count, own_ref, fold_ref, *refs):
    dk_ref, dv_ref = refs[len(sets) :]
    me = lax.axis_index("ctx")
    length = own_ref.shape[0] // 2
    width = dk_ref.shape[1]
    low = own_ref[:length, :] + fold_ref[...]
    up = own_ref[length:, :]
    for entry, ref in zip(sets, refs):
        offset = entry["offset"]
        first = (me // offset) % 2 == entry["colour"]
        as_first = first & (me + offset < ctx_count)
        as_second = jnp.logical_not(first) & (me >= offset)
        if entry["full"]:
            low = low + jnp.where(as_first | as_second, ref[:length, :].astype(jnp.float32), 0.0)
            up = up + jnp.where(as_second, ref[length:, :].astype(jnp.float32), 0.0)
        else:
            part = ref[...].astype(jnp.float32)
            for pair in entry["folds"]:
                as_first = as_first & (me != pair[0]) | (me == pair[1])
            low = low + jnp.where(as_first, part, 0.0)
            up = up + jnp.where(as_second, part, 0.0)
    dk_ref[:length, :] = low[:, :width].astype(jnp.bfloat16)
    dk_ref[length:, :] = up[:, :width].astype(jnp.bfloat16)
    dv_ref[:length, :] = low[:, width:].astype(jnp.bfloat16)
    dv_ref[length:, :] = up[:, width:].astype(jnp.bfloat16)


def in_vmem(amount):
    return [pl.BlockSpec(memory_space=pltpu.VMEM)] * amount


def in_place(amount):
    return [pl.BlockSpec(memory_space=pl.ANY)] * amount


def on_chip(values):
    return [pltpu.with_memory_space_constraint(v, pltpu.VMEM) for v in values]


def off_chip(values):
    return [pltpu.with_memory_space_constraint(v, pltpu.HBM) for v in values]


def shards(query_rows, key_rows, value_rows, out_grad, doc_lengths):
    ctx_count = lax.axis_size("ctx")
    head_count = lax.axis_size("head")
    tok_dev = query_rows.shape[0]
    length = tok_dev // 2
    width = key_rows.shape[1]
    reach = min(DOC_STRETCHES, ctx_count // 4)
    span = (reach + 1) * length
    heads = query_rows.shape[1] // width
    sets = exchanges(ctx_count, reach)
    fulls = sum(s["full"] for s in sets)
    count = len(sets)
    payloads = [
        pltpu.VMEM((2 * length if s["full"] else length, 2 * width), jnp.bfloat16) for s in sets
    ]
    mine, *halves = pl.pallas_call(
        lambda *refs: pack_kernel(sets, *refs),
        out_shape=[pltpu.VMEM((tok_dev, 2 * width), jnp.bfloat16)] + payloads[fulls:],
        in_specs=in_place(2),
        out_specs=in_vmem(1 + count - fulls),
        scratch_shapes=[pltpu.SemaphoreType.DMA((2 + 2 * (count - fulls),))],
        compiler_params=pltpu.CompilerParams(vmem_limit_bytes=VMEM_LIMIT),
        name="pack",
    )(*off_chip([key_rows, value_rows]))
    packed = [mine] * fulls + halves
    received = [swap(p, s, ctx_count, head_count, "fetch") for p, s in zip(packed, sets)]

    stack = pltpu.VMEM((heads, tok_dev, width), jnp.bfloat16)
    q_all, g_all, bias = pl.pallas_call(
        lambda *refs: stage_kernel(ctx_count, *refs),
        out_shape=[stack, stack, pltpu.VMEM((2, reach * length, length), jnp.float32)],
        in_specs=in_place(3),
        out_specs=in_vmem(3),
        scratch_shapes=[
            pltpu.SMEM(doc_lengths.shape, jnp.int32),
            pltpu.SemaphoreType.DMA((3, heads)),
        ],
        compiler_params=pltpu.CompilerParams(vmem_limit_bytes=VMEM_LIMIT),
        name="stage",
    )(*off_chip([doc_lengths, query_rows, out_grad]))

    low_weights = pltpu.VMEM((2, heads, span, length), jnp.bfloat16)
    pb, dsb, kv_win, folded, *partials = pl.pallas_call(
        lambda *refs: score_kernel(sets, ctx_count, reach, *refs),
        out_shape=[
            low_weights,
            low_weights,
            pltpu.VMEM((2, span, 2 * width), jnp.bfloat16),
            pltpu.VMEM((length, 2 * width), jnp.float32),
        ]
        + payloads,
        in_specs=in_vmem(4 + count),
        out_specs=in_vmem(4 + count),
        scratch_shapes=[
            pltpu.VMEM((2, span, 2 * width), jnp.float32),
            pltpu.VMEM((reach * length, 2 * width), jnp.float32),
        ],
        compiler_params=pltpu.CompilerParams(vmem_limit_bytes=VMEM_LIMIT),
        name="score",
    )(*on_chip([bias, q_all, g_all, mine, *received]))
    returned = [swap(p, s, ctx_count, head_count, "give") for p, s in zip(partials, sets)]

    attended, query_grad, own = pl.pallas_call(
        output_kernel,
        out_shape=[jax.ShapeDtypeStruct(query_rows.shape, jnp.bfloat16)] * 2
        + [pltpu.VMEM((tok_dev, 2 * width), jnp.float32)],
        in_specs=in_vmem(5),
        out_specs=in_place(2) + in_vmem(1),
        scratch_shapes=[
            pltpu.VMEM(query_rows.shape, jnp.bfloat16),
            pltpu.VMEM(query_rows.shape, jnp.bfloat16),
            pltpu.SemaphoreType.DMA((2, 2)),
        ],
        compiler_params=pltpu.CompilerParams(vmem_limit_bytes=VMEM_LIMIT),
        name="output",
    )(*on_chip([pb, dsb, kv_win, q_all, g_all]))

    key_grad, value_grad = pl.pallas_call(
        lambda *refs: sum_kernel(sets, ctx_count, *refs),
        out_shape=[jax.ShapeDtypeStruct(key_rows.shape, jnp.bfloat16)] * 2,
        in_specs=in_vmem(2 + count),
        out_specs=in_vmem(2),
        compiler_params=pltpu.CompilerParams(vmem_limit_bytes=VMEM_LIMIT),
        name="total",
    )(*on_chip([own, folded, *returned]))
    return (attended, query_grad, key_grad, value_grad)


def solution(mesh):
    placed = (
        P(("groups", "ctx"), "head"),
        P(("groups", "ctx"), "head"),
        P(("groups", "ctx"), "head"),
        P(("groups", "ctx"), "head"),
        P("groups"),
    )
    return jax.shard_map(
        shards,
        mesh=mesh,
        in_specs=placed,
        out_specs=(P(("groups", "ctx"), "head"),) * 4,
        check_vma=False,
    )
```

```python
import math

import jax
import jax.numpy as jnp
from jax import lax
from jax.experimental import pallas as pl
from jax.experimental.pallas import tpu as pltpu
from jax.sharding import PartitionSpec as P

HEAD_DIM = 128
DOC_STRETCHES = 8
MASKED = -1e30
VMEM_LIMIT = 24 << 20


def exchanges(ctx_count, reach):
    sets = []
    for offset in range(1, reach + 1):
        for colour in range(2):
            firsts = [b for b in range(ctx_count - offset) if (b // offset) % 2 == colour]
            if firsts:
                sets.append(dict(offset=offset, colour=colour, full=False, firsts=firsts, folds=[]))
    while not place_folds(sets, ctx_count, reach):
        pass
    return sorted(sets, key=lambda entry: not entry["full"])


def place_folds(sets, ctx_count, reach):
    for entry in sets:
        entry["folds"] = []
    for entry in sets:
        offset = entry["offset"]
        for b in entry["firsts"]:
            if entry["full"] or 2 * b < 2 * ctx_count - 1 - reach - offset:
                continue
            for other in sets:
                busy = [x for f in other["firsts"] for x in (f, f + other["offset"])]
                busy += [x for pair in other["folds"] for x in pair]
                sends_low = ((b + offset) // other["offset"]) % 2 == other["colour"]
                if b not in busy and b + offset not in busy and sends_low and not other["full"]:
                    other["folds"].append((b, b + offset))
                    break
            else:
                entry["full"] = True
                return False
    return True


def key_of(entry):
    return entry["offset"], entry["colour"]


def swap(value, exchange, ctx_count, head_count, phase):
    partner = {}
    pairs = [(b, b + exchange["offset"]) for b in exchange["firsts"]] + exchange["folds"]
    for a, b in pairs:
        partner[a], partner[b] = b, a
    pairs = []
    for b in range(ctx_count):
        for h in range(head_count):
            if b in partner:
                pairs.append((b * head_count + h, partner[b] * head_count + h))
            else:
                pairs.append((b * head_count + h, b * head_count + (h + 1) % head_count))
    with jax.named_scope(f"{phase}_{exchange['offset']}_{exchange['colour']}"):
        return lax.ppermute(value, ("ctx", "head"), pairs)


def fold_offsets(slot):
    return range(-(slot - 1), slot, 2)


def pack_kernel(sets, k_hbm, v_hbm, mine, *refs):
    halves = [s for s in sets if not s["full"]]
    outs, sems = refs[: len(halves)], refs[len(halves)]
    me = lax.axis_index("ctx")
    length = k_hbm.shape[0] // 2
    width = k_hbm.shape[1]
    copies = [
        pltpu.make_async_copy(k_hbm, mine.at[:, :width], sems.at[0]),
        pltpu.make_async_copy(v_hbm, mine.at[:, width:], sems.at[1]),
    ]
    for i, (entry, out) in enumerate(zip(halves, outs)):
        first = (me // entry["offset"]) % 2 == entry["colour"]
        rows = pl.ds(pl.multiple_of(jnp.where(first, 0, length), length), length)
        copies.append(pltpu.make_async_copy(k_hbm.at[rows, :], out.at[:, :width], sems.at[2 * i + 2]))
        copies.append(pltpu.make_async_copy(v_hbm.at[rows, :], out.at[:, width:], sems.at[2 * i + 3]))
    for copy in copies:
        copy.start()
    for copy in copies:
        copy.wait()


def stage_kernel(ctx_count, docs_hbm, q_hbm, g_hbm, q_all, g_all, bias, docs_ref, sems):
    length = q_hbm.shape[0] // 2
    heads, _, width = q_all.shape
    lengths = pltpu.make_async_copy(docs_hbm, docs_ref, sems.at[2, 0])
    lengths.start()
    copies = []
    for h in range(heads):
        cols = slice(h * width, (h + 1) * width)
        for a, (src, dst) in enumerate(((q_hbm, q_all), (g_hbm, g_all))):
            copies.append(pltpu.make_async_copy(src.at[:, cols], dst.at[h], sems.at[a, h]))
    for copy in copies:
        copy.start()
    lengths.wait()
    me = lax.axis_index("ctx")
    merged = bias.shape[1]
    row = lax.broadcasted_iota(jnp.int32, (merged, length), 0)
    col = lax.broadcasted_iota(jnp.int32, (1, length), 1)
    for s in range(2):
        stretch = me if s == 0 else 2 * ctx_count - 1 - me
        q_pos = stretch * length + col
        start = jnp.int32(0)
        doc_start = jnp.zeros((1, length), jnp.int32)
        for i in range(docs_ref.shape[0]):
            doc_start = jnp.where(q_pos >= start, start, doc_start)
            start = start + docs_ref[i]
        k_pos = row + (stretch - 2 * (row // length)) * length
        k_pos = jnp.where(k_pos > q_pos, k_pos - merged, k_pos)
        bias[s] = jnp.where(k_pos >= doc_start, 0.0, MASKED)
    for copy in copies:
        copy.wait()


def stacked(ref, s, first=0, last=None):
    length = ref.shape[1] // 2
    value = ref[first:last, s * length : (s + 1) * length, :]
    return value.reshape(-1, ref.shape[2])


def unfolded(ref, s, h, near_low):
    length = ref.shape[3]
    value = ref[s, h]
    own = value[:length, :] * near_low
    return jnp.concatenate([own, value[length:, :], value[:length, :] - own], axis=0)


def score_kernel(sets, ctx_count, reach, bias, q_all, g_all, mine, *refs):
    count = len(sets)
    recs = {key_of(s): (r, s["full"]) for s, r in zip(sets, refs[:count])}
    pb, dsb, kv_win, own_ref = refs[count : count + 4]
    send_refs = refs[count + 4 : 2 * count + 4]
    acc, extra = refs[2 * count + 4 :]
    me = lax.axis_index("ctx")
    length = mine.shape[0] // 2
    width = HEAD_DIM
    heads = q_all.shape[0]
    merged = reach * length
    scaling = width ** (-0.5)
    log_scale = scaling * math.log2(math.e)

    def low_part(key):
        ref, full = recs[key]
        return ref[:length, :] if full else ref[...]

    def up_part(key):
        ref, full = recs[key]
        return ref[length:, :] if full else ref[...]

    def pick(part, offset, colour_pred):
        have = [c for c in range(2) if (offset, c) in recs]
        if len(have) == 1:
            return part((offset, have[0]))
        return jnp.where(colour_pred, part((offset, 1)), part((offset, 0)))

    lows = [mine[:length, :]]
    highs = [mine[length:, :]]
    for slot in range(1, reach + 1):
        odd = (me // slot) % 2 == 1
        lows.append(pick(low_part, slot, jnp.logical_not(odd)))
        highs.append(pick(up_part, slot, odd))
    for slot in range(1, reach + 1):
        folded = me + slot >= ctx_count
        value = highs[slot]
        for offset in fold_offsets(slot):
            here = folded & (2 * ctx_count - 1 - 2 * me - slot == offset)
            if offset <= 0:
                value = jnp.where(here, lows[-offset], value)
            else:
                for colour in range(2):
                    if recs.get((offset, colour), (None, False))[1]:
                        where = here & ((me // offset) % 2 == colour)
                        value = jnp.where(where, low_part((offset, colour)), value)
                for entry in sets:
                    for pair in entry["folds"]:
                        if pair[1] - pair[0] == offset:
                            where = here & (me == pair[0])
                            value = jnp.where(where, recs[key_of(entry)][0][...], value)
        highs[slot] = value
    for slot in range(reach + 1):
        rows = slice(slot * length, (slot + 1) * length)
        kv_win[0, rows, :] = lows[slot]
        kv_win[1, rows, :] = highs[slot]

    tri_row = lax.broadcasted_iota(jnp.int32, (length, length), 0)
    near = tri_row <= lax.broadcasted_iota(jnp.int32, (length, length), 1)
    far_low = jnp.where(near, 0.0, 1.0).astype(jnp.bfloat16)

    def fold(value):
        return jnp.where(near, value[:length, :], value[merged:, :])

    def products(s, h):
        contract_last = (((1,), (1,)), ((), ()))
        raw = lax.dot_general(
            kv_win[s, :, :width],
            stacked(q_all, s, h, h + group),
            contract_last,
            preferred_element_type=jnp.float32,
        )
        d_p = lax.dot_general(
            kv_win[s, :, width:],
            stacked(g_all, s, h, h + group),
            contract_last,
            preferred_element_type=jnp.float32,
        )
        return raw, d_p

    def soften(s, h, raw, d_p):
        raw = jnp.concatenate([fold(raw), raw[length:merged, :]], axis=0) + bias[s]
        d_p = jnp.concatenate([fold(d_p), d_p[length:merged, :]], axis=0)
        top = jnp.max(raw, axis=0, keepdims=True)
        weight = jnp.exp2((raw - top) * log_scale)
        total = jnp.sum(weight, axis=0, keepdims=True)
        inverse = 1.0 / total
        delta = jnp.sum(weight * d_p, axis=0, keepdims=True) * inverse
        weight = weight * inverse
        others = []
        for ref, value in ((pb, weight), (dsb, weight * (d_p - delta))):
            value = value.astype(jnp.bfloat16)
            ref[s, h] = value
            others.append(jnp.concatenate([value[length:, :], value[:length, :] * far_low], axis=0))
        return others

    def gradients(s, first, last, done):
        part = slice(length, None)
        weights, d_scores = [jnp.concatenate(values, axis=1) for values in zip(*done)]
        d_k = jnp.dot(
            d_scores, stacked(q_all, s, first, last), preferred_element_type=jnp.float32
        )
        d_v = jnp.dot(weights, stacked(g_all, s, first, last), preferred_element_type=jnp.float32)
        if first > 0:
            d_k = d_k + acc[s, part, :width]
            d_v = d_v + acc[s, part, width:]
        if last == heads:
            d_k = d_k * scaling
        acc[s, part, :width] = d_k
        acc[s, part, width:] = d_v

    group = 2 if heads % 2 == 0 else 1
    items = [(s, h) for s in range(2) for h in range(0, heads, group)]
    stops = [{heads // 2, heads}, {heads - group, heads}]
    done = []
    ready = products(*items[0])
    for i, (s, h) in enumerate(items):
        following = products(*items[i + 1]) if i + 1 < len(items) else None
        for j in range(group):
            part = slice(j * length, (j + 1) * length)
            done.append(soften(s, h + j, ready[0][:, part], ready[1][:, part]))
        ready = following
        if h + group in stops[s]:
            gradients(s, h + group - len(done), h + group, done)
            done = []

    def slot_rows(slot):
        return slice(slot * length, (slot + 1) * length)

    extra[...] = jnp.zeros(extra.shape, jnp.float32)
    for slot in range(1, reach + 1):
        for offset in fold_offsets(slot):

            @pl.when((me + slot >= ctx_count) & (2 * ctx_count - 1 - 2 * me - slot == offset))
            def _():
                part = acc[1, slot_rows(slot), :]
                if offset < 0:
                    acc[0, slot_rows(-offset), :] = acc[0, slot_rows(-offset), :] + part
                else:
                    extra[slot_rows(offset), :] = part

    own_ref[...] = extra[:length, :]
    for entry, ref in zip(sets, send_refs):
        offset = entry["offset"]
        first = (me // offset) % 2 == entry["colour"]
        side = jnp.where(first, 1, 0)
        if entry["full"]:
            to_low = acc[0, slot_rows(offset), :]
            to_up = acc[1, slot_rows(offset), :]
            more = extra[slot_rows(offset), :]
            ref[:length, :] = jnp.where(first, more, to_low).astype(jnp.bfloat16)
            ref[length:, :] = jnp.where(first, to_up, 0.0).astype(jnp.bfloat16)
        else:
            part = acc[side, slot_rows(offset), :]
            for pair in entry["folds"]:
                part = jnp.where(me == pair[0], extra[slot_rows(pair[1] - pair[0]), :], part)
            ref[...] = part.astype(jnp.bfloat16)


def output_kernel(pb, dsb, kv_win, q_all, g_all, att_hbm, dq_hbm, own_ref, att, dq, sems):
    length = att.shape[0] // 2
    width = HEAD_DIM
    heads = att.shape[1] // width
    scaling = width ** (-0.5)
    group = 2 if heads % 2 == 0 else 1
    tri_row = lax.broadcasted_iota(jnp.int32, (length, length), 0)
    tri_col = lax.broadcasted_iota(jnp.int32, (length, length), 1)
    near_low = jnp.where(tri_row <= tri_col, 1.0, 0.0).astype(jnp.bfloat16)
    copies = []
    for s in range(2):
        rows = slice(s * length, (s + 1) * length)
        k_turn = kv_win[s, :, :width].T
        v_turn = kv_win[s, :, width:].T
        own_weights, own_scores = [], []
        for h in range(0, heads, group):
            weights = [unfolded(pb, s, h + i, near_low) for i in range(group)]
            d_scores = [unfolded(dsb, s, h + i, near_low) for i in range(group)]
            own_weights += [value[:length, :] for value in weights]
            own_scores += [value[:length, :] for value in d_scores]
            out_t = jnp.dot(
                v_turn, jnp.concatenate(weights, axis=1), preferred_element_type=jnp.float32
            )
            dq_t = jnp.dot(
                k_turn, jnp.concatenate(d_scores, axis=1), preferred_element_type=jnp.float32
            )
            out_t = out_t.astype(jnp.bfloat16)
            dq_t = (dq_t * scaling).astype(jnp.bfloat16)
            for i in range(group):
                part = slice(i * length, (i + 1) * length)
                cols = slice((h + i) * width, (h + i + 1) * width)
                att[rows, cols] = out_t[:, part].T
                dq[rows, cols] = dq_t[:, part].T
        for a, (src, dst) in enumerate(((att, att_hbm), (dq, dq_hbm))):
            copy = pltpu.make_async_copy(src.at[rows, :], dst.at[rows, :], sems.at[s, a])
            copy.start()
            copies.append(copy)
        d_k = jnp.dot(
            jnp.concatenate(own_scores, axis=1),
            stacked(q_all, s),
            preferred_element_type=jnp.float32,
        )
        d_v = jnp.dot(
            jnp.concatenate(own_weights, axis=1),
            stacked(g_all, s),
            preferred_element_type=jnp.float32,
        )
        own_ref[rows, :width] = d_k * scaling
        own_ref[rows, width:] = d_v
    for copy in copies:
        copy.wait()


def sum_kernel(sets, ctx_count, own_ref, fold_ref, *refs):
    dk_ref, dv_ref = refs[len(sets) :]
    me = lax.axis_index("ctx")
    length = own_ref.shape[0] // 2
    width = dk_ref.shape[1]
    low = own_ref[:length, :] + fold_ref[...]
    up = own_ref[length:, :]
    for entry, ref in zip(sets, refs):
        offset = entry["offset"]
        first = (me // offset) % 2 == entry["colour"]
        as_first = first & (me + offset < ctx_count)
        as_second = jnp.logical_not(first) & (me >= offset)
        if entry["full"]:
            low = low + jnp.where(as_first | as_second, ref[:length, :].astype(jnp.float32), 0.0)
            up = up + jnp.where(as_second, ref[length:, :].astype(jnp.float32), 0.0)
        else:
            part = ref[...].astype(jnp.float32)
            for pair in entry["folds"]:
                as_first = as_first & (me != pair[0]) | (me == pair[1])
            low = low + jnp.where(as_first, part, 0.0)
            up = up + jnp.where(as_second, part, 0.0)
    dk_ref[:length, :] = low[:, :width].astype(jnp.bfloat16)
    dk_ref[length:, :] = up[:, :width].astype(jnp.bfloat16)
    dv_ref[:length, :] = low[:, width:].astype(jnp.bfloat16)
    dv_ref[length:, :] = up[:, width:].astype(jnp.bfloat16)


def in_vmem(amount):
    return [pl.BlockSpec(memory_space=pltpu.VMEM)] * amount


def in_place(amount):
    return [pl.BlockSpec(memory_space=pl.ANY)] * amount


def on_chip(values):
    return [pltpu.with_memory_space_constraint(v, pltpu.VMEM) for v in values]


def off_chip(values):
    return [pltpu.with_memory_space_constraint(v, pltpu.HBM) for v in values]


def shards(query_rows, key_rows, value_rows, out_grad, doc_lengths):
    ctx_count = lax.axis_size("ctx")
    head_count = lax.axis_size("head")
    tok_dev = query_rows.shape[0]
    length = tok_dev // 2
    width = key_rows.shape[1]
    reach = min(DOC_STRETCHES, ctx_count // 4)
    span = (reach + 1) * length
    heads = query_rows.shape[1] // width
    sets = exchanges(ctx_count, reach)
    fulls = sum(s["full"] for s in sets)
    count = len(sets)
    payloads = [
        pltpu.VMEM((2 * length if s["full"] else length, 2 * width), jnp.bfloat16) for s in sets
    ]
    mine, *halves = pl.pallas_call(
        lambda *refs: pack_kernel(sets, *refs),
        out_shape=[pltpu.VMEM((tok_dev, 2 * width), jnp.bfloat16)] + payloads[fulls:],
        in_specs=in_place(2),
        out_specs=in_vmem(1 + count - fulls),
        scratch_shapes=[pltpu.SemaphoreType.DMA((2 + 2 * (count - fulls),))],
        compiler_params=pltpu.CompilerParams(vmem_limit_bytes=VMEM_LIMIT),
        name="pack",
    )(*off_chip([key_rows, value_rows]))
    packed = [mine] * fulls + halves
    received = [swap(p, s, ctx_count, head_count, "fetch") for p, s in zip(packed, sets)]

    stack = pltpu.VMEM((heads, tok_dev, width), jnp.bfloat16)
    q_all, g_all, bias = pl.pallas_call(
        lambda *refs: stage_kernel(ctx_count, *refs),
        out_shape=[stack, stack, pltpu.VMEM((2, reach * length, length), jnp.float32)],
        in_specs=in_place(3),
        out_specs=in_vmem(3),
        scratch_shapes=[
            pltpu.SMEM(doc_lengths.shape, jnp.int32),
            pltpu.SemaphoreType.DMA((3, heads)),
        ],
        compiler_params=pltpu.CompilerParams(vmem_limit_bytes=VMEM_LIMIT),
        name="stage",
    )(*off_chip([doc_lengths, query_rows, out_grad]))

    low_weights = pltpu.VMEM((2, heads, reach * length, length), jnp.bfloat16)
    pb, dsb, kv_win, folded, *partials = pl.pallas_call(
        lambda *refs: score_kernel(sets, ctx_count, reach, *refs),
        out_shape=[
            low_weights,
            low_weights,
            pltpu.VMEM((2, span, 2 * width), jnp.bfloat16),
            pltpu.VMEM((length, 2 * width), jnp.float32),
        ]
        + payloads,
        in_specs=in_vmem(4 + count),
        out_specs=in_vmem(4 + count),
        scratch_shapes=[
            pltpu.VMEM((2, span, 2 * width), jnp.float32),
            pltpu.VMEM((reach * length, 2 * width), jnp.float32),
        ],
        compiler_params=pltpu.CompilerParams(vmem_limit_bytes=VMEM_LIMIT),
        name="score",
    )(*on_chip([bias, q_all, g_all, mine, *received]))
    returned = [swap(p, s, ctx_count, head_count, "give") for p, s in zip(partials, sets)]

    attended, query_grad, own = pl.pallas_call(
        output_kernel,
        out_shape=[jax.ShapeDtypeStruct(query_rows.shape, jnp.bfloat16)] * 2
        + [pltpu.VMEM((tok_dev, 2 * width), jnp.float32)],
        in_specs=in_vmem(5),
        out_specs=in_place(2) + in_vmem(1),
        scratch_shapes=[
            pltpu.VMEM(query_rows.shape, jnp.bfloat16),
            pltpu.VMEM(query_rows.shape, jnp.bfloat16),
            pltpu.SemaphoreType.DMA((2, 2)),
        ],
        compiler_params=pltpu.CompilerParams(vmem_limit_bytes=VMEM_LIMIT),
        name="output",
    )(*on_chip([pb, dsb, kv_win, q_all, g_all]))

    key_grad, value_grad = pl.pallas_call(
        lambda *refs: sum_kernel(sets, ctx_count, *refs),
        out_shape=[jax.ShapeDtypeStruct(key_rows.shape, jnp.bfloat16)] * 2,
        in_specs=in_vmem(2 + count),
        out_specs=in_vmem(2),
        compiler_params=pltpu.CompilerParams(vmem_limit_bytes=VMEM_LIMIT),
        name="total",
    )(*on_chip([own, folded, *returned]))
    return (attended, query_grad, key_grad, value_grad)


def solution(mesh):
    placed = (
        P(("groups", "ctx"), "head"),
        P(("groups", "ctx"), "head"),
        P(("groups", "ctx"), "head"),
        P(("groups", "ctx"), "head"),
        P("groups"),
    )
    return jax.shard_map(
        shards,
        mesh=mesh,
        in_specs=placed,
        out_specs=(P(("groups", "ctx"), "head"),) * 4,
        check_vma=False,
    )
```

```python
import math

import jax
import jax.numpy as jnp
from jax import lax
from jax.experimental import pallas as pl
from jax.experimental.pallas import tpu as pltpu
from jax.sharding import PartitionSpec as P

HEAD_DIM = 128
DOC_STRETCHES = 8
MASKED = -1e30
VMEM_LIMIT = 24 << 20


def exchanges(ctx_count, reach):
    sets = []
    for offset in range(1, reach + 1):
        for colour in range(2):
            firsts = [b for b in range(ctx_count - offset) if (b // offset) % 2 == colour]
            if firsts:
                sets.append(dict(offset=offset, colour=colour, full=False, firsts=firsts, folds=[]))
    while not place_folds(sets, ctx_count, reach):
        pass
    return sorted(sets, key=lambda entry: not entry["full"])


def place_folds(sets, ctx_count, reach):
    for entry in sets:
        entry["folds"] = []
    for entry in sets:
        offset = entry["offset"]
        for b in entry["firsts"]:
            if entry["full"] or 2 * b < 2 * ctx_count - 1 - reach - offset:
                continue
            for other in sets:
                busy = [x for f in other["firsts"] for x in (f, f + other["offset"])]
                busy += [x for pair in other["folds"] for x in pair]
                sends_low = ((b + offset) // other["offset"]) % 2 == other["colour"]
                if b not in busy and b + offset not in busy and sends_low and not other["full"]:
                    other["folds"].append((b, b + offset))
                    break
            else:
                entry["full"] = True
                return False
    return True


def key_of(entry):
    return entry["offset"], entry["colour"]


def swap(value, exchange, ctx_count, head_count, phase):
    partner = {}
    pairs = [(b, b + exchange["offset"]) for b in exchange["firsts"]] + exchange["folds"]
    for a, b in pairs:
        partner[a], partner[b] = b, a
    pairs = []
    for b in range(ctx_count):
        for h in range(head_count):
            if b in partner:
                pairs.append((b * head_count + h, partner[b] * head_count + h))
            else:
                pairs.append((b * head_count + h, b * head_count + (h + 1) % head_count))
    with jax.named_scope(f"{phase}_{exchange['offset']}_{exchange['colour']}"):
        return lax.ppermute(value, ("ctx", "head"), pairs)


def fold_offsets(slot):
    return range(-(slot - 1), slot, 2)


def pack_kernel(sets, k_hbm, v_hbm, mine, *refs):
    halves = [s for s in sets if not s["full"]]
    outs, sems = refs[: len(halves)], refs[len(halves)]
    me = lax.axis_index("ctx")
    length = k_hbm.shape[0] // 2
    width = k_hbm.shape[1]
    copies = [
        pltpu.make_async_copy(k_hbm, mine.at[:, :width], sems.at[0]),
        pltpu.make_async_copy(v_hbm, mine.at[:, width:], sems.at[1]),
    ]
    for i, (entry, out) in enumerate(zip(halves, outs)):
        first = (me // entry["offset"]) % 2 == entry["colour"]
        rows = pl.ds(pl.multiple_of(jnp.where(first, 0, length), length), length)
        copies.append(pltpu.make_async_copy(k_hbm.at[rows, :], out.at[:, :width], sems.at[2 * i + 2]))
        copies.append(pltpu.make_async_copy(v_hbm.at[rows, :], out.at[:, width:], sems.at[2 * i + 3]))
    for copy in copies:
        copy.start()
    for copy in copies:
        copy.wait()


def stage_kernel(ctx_count, docs_hbm, q_hbm, g_hbm, q_all, g_all, bias, docs_ref, sems):
    length = q_hbm.shape[0] // 2
    heads, _, width = q_all.shape
    lengths = pltpu.make_async_copy(docs_hbm, docs_ref, sems.at[2, 0])
    lengths.start()
    copies = []
    for h in range(heads):
        cols = slice(h * width, (h + 1) * width)
        for a, (src, dst) in enumerate(((q_hbm, q_all), (g_hbm, g_all))):
            copies.append(pltpu.make_async_copy(src.at[:, cols], dst.at[h], sems.at[a, h]))
    for copy in copies:
        copy.start()
    lengths.wait()
    me = lax.axis_index("ctx")
    merged = bias.shape[2]
    row = lax.broadcasted_iota(jnp.int32, (merged, length), 0)
    half = length // 2
    col = lax.broadcasted_iota(jnp.int32, (1, length), 1) % half
    for s, u in ((0, 0), (0, 1), (1, 0), (1, 1)):
        stretch = me if s == 0 else 2 * ctx_count - 1 - me
        q_pos = stretch * length + u * half + col
        start = jnp.int32(0)
        doc_start = jnp.zeros((1, length), jnp.int32)
        for i in range(docs_ref.shape[0]):
            doc_start = jnp.where(q_pos >= start, start, doc_start)
            start = start + docs_ref[i]
        k_pos = row + (stretch - 2 * (row // length)) * length
        k_pos = jnp.where(k_pos > q_pos, k_pos - merged, k_pos)
        bias[s, u] = jnp.where(k_pos >= doc_start, 0.0, MASKED)
    for copy in copies:
        copy.wait()


def stacked(ref, s, u, first=0, last=None):
    half = ref.shape[1] // 4
    start = (2 * s + u) * half
    return ref[first:last, start : start + half, :].reshape(-1, ref.shape[2])


def unfolded(ref, s, h, near_low):
    length = ref.shape[3]
    value = ref[s, h]
    own = value[:length, :] * near_low
    return jnp.concatenate([own, value[length:, :], value[:length, :] - own], axis=0)


def score_kernel(sets, ctx_count, reach, bias, q_all, g_all, mine, *refs):
    count = len(sets)
    recs = {key_of(s): (r, s["full"]) for s, r in zip(sets, refs[:count])}
    pb, dsb, kv_win, own_ref = refs[count : count + 4]
    send_refs = refs[count + 4 : 2 * count + 4]
    acc, extra = refs[2 * count + 4 :]
    me = lax.axis_index("ctx")
    length = mine.shape[0] // 2
    width = HEAD_DIM
    heads = q_all.shape[0]
    merged = reach * length
    scaling = width ** (-0.5)
    log_scale = scaling * math.log2(math.e)

    def low_part(key):
        ref, full = recs[key]
        return ref[:length, :] if full else ref[...]

    def up_part(key):
        ref, full = recs[key]
        return ref[length:, :] if full else ref[...]

    def pick(part, offset, colour_pred):
        have = [c for c in range(2) if (offset, c) in recs]
        if len(have) == 1:
            return part((offset, have[0]))
        return jnp.where(colour_pred, part((offset, 1)), part((offset, 0)))

    lows = [mine[:length, :]]
    highs = [mine[length:, :]]
    for slot in range(1, reach + 1):
        odd = (me // slot) % 2 == 1
        lows.append(pick(low_part, slot, jnp.logical_not(odd)))
        highs.append(pick(up_part, slot, odd))
    for slot in range(1, reach + 1):
        folded = me + slot >= ctx_count
        value = highs[slot]
        for offset in fold_offsets(slot):
            here = folded & (2 * ctx_count - 1 - 2 * me - slot == offset)
            if offset <= 0:
                value = jnp.where(here, lows[-offset], value)
            else:
                for colour in range(2):
                    if recs.get((offset, colour), (None, False))[1]:
                        where = here & ((me // offset) % 2 == colour)
                        value = jnp.where(where, low_part((offset, colour)), value)
                for entry in sets:
                    for pair in entry["folds"]:
                        if pair[1] - pair[0] == offset:
                            where = here & (me == pair[0])
                            value = jnp.where(where, recs[key_of(entry)][0][...], value)
        highs[slot] = value
    for slot in range(reach + 1):
        rows = slice(slot * length, (slot + 1) * length)
        kv_win[0, rows, :] = lows[slot]
        kv_win[1, rows, :] = highs[slot]

    half = length // 2
    group = next(g for g in (4, 2) if heads % g == 0)
    lanes = 2 * half
    tri_row = lax.broadcasted_iota(jnp.int32, (half, lanes), 0)
    near = tri_row <= lax.broadcasted_iota(jnp.int32, (half, lanes), 1) % half
    far_low = jnp.where(near, 0.0, 1.0).astype(jnp.bfloat16)
    contract_last = (((1,), (1,)), ((), ()))

    def products(s, u, h):
        own_rows = slice(0, length if u else half)
        last_rows = slice(merged + half if u else merged, None)

        def window(cols):
            parts = [kv_win[s, own_rows, cols], kv_win[s, length:merged, cols]]
            return jnp.concatenate(parts + [kv_win[s, last_rows, cols]], axis=0)

        raw = lax.dot_general(
            window(slice(0, width)),
            stacked(q_all, s, u, h, h + group),
            contract_last,
            preferred_element_type=jnp.float32,
        )
        d_p = lax.dot_general(
            window(slice(width, None)),
            stacked(g_all, s, u, h, h + group),
            contract_last,
            preferred_element_type=jnp.float32,
        )
        return raw, d_p

    def fold(u, value):
        if u:
            top = value[:half, :]
            low = jnp.where(near, value[half:length, :], value[merged:, :])
            middle = value[length:merged, :]
        else:
            last = value[merged - half :, :]
            top = jnp.where(near, value[:half, :], last[:half, :])
            low = last[half:, :]
            middle = value[half : merged - half, :]
        return jnp.concatenate([top, low, middle], axis=0)

    def soften(s, u, block, raw, d_p):
        raw = fold(u, raw) + bias[s, u]
        d_p = fold(u, d_p)
        top = jnp.max(raw, axis=0, keepdims=True)
        weight = jnp.exp2((raw - top) * log_scale)
        total = jnp.sum(weight, axis=0, keepdims=True)
        inverse = 1.0 / total
        delta = jnp.sum(weight * d_p, axis=0, keepdims=True) * inverse
        weight = weight * inverse
        others = []
        for ref, value in ((pb, weight), (dsb, weight * (d_p - delta))):
            value = value.astype(jnp.bfloat16)
            ref[s, block] = value
            if u:
                last = [value[half:length, :] * far_low]
            else:
                last = [value[:half, :] * far_low, value[half:length, :]]
            others.append(jnp.concatenate([value[length:, :]] + last, axis=0))
        return others

    def gradients(s, u, first, last, start, done):
        weights, d_scores = [jnp.concatenate(values, axis=1) for values in zip(*done)]
        parts = [(slice(length, merged), slice(0, merged - length))] if merged > length else []
        parts.append((slice(merged + u * half, merged + length), slice(merged - length, None)))
        for cols, left, right in (
            (slice(0, width), d_scores, q_all),
            (slice(width, None), weights, g_all),
        ):
            value = jnp.dot(
                left, stacked(right, s, u, first, last), preferred_element_type=jnp.float32
            )
            if right is q_all:
                value = value * scaling
            for rows, part in parts:
                if start:
                    acc[s, rows, cols] = value[part, :]
                else:
                    acc[s, rows, cols] = acc[s, rows, cols] + value[part, :]

    items = [(s, u, h) for s in range(2) for u in range(2) for h in range(0, heads, group)]
    done = []
    ready = products(*items[0])
    for i, (s, u, h) in enumerate(items):
        following = products(*items[i + 1]) if i + 1 < len(items) else None
        for j in range(0, group, 2):
            part = slice(j // 2 * lanes, (j // 2 + 1) * lanes)
            block = (u * heads + h + j) // 2
            done.append(soften(s, u, block, ready[0][:, part], ready[1][:, part]))
        ready = following
        last = h + group
        if last == heads or (s, u) == (1, 1) and last == heads - group:
            first = last - 2 * len(done)
            gradients(s, u, first, last, u == 0, done)
            done = []

    def slot_rows(slot):
        return slice(slot * length, (slot + 1) * length)

    extra[...] = jnp.zeros(extra.shape, jnp.float32)
    for slot in range(1, reach + 1):
        for offset in fold_offsets(slot):

            @pl.when((me + slot >= ctx_count) & (2 * ctx_count - 1 - 2 * me - slot == offset))
            def _():
                part = acc[1, slot_rows(slot), :]
                if offset < 0:
                    acc[0, slot_rows(-offset), :] = acc[0, slot_rows(-offset), :] + part
                else:
                    extra[slot_rows(offset), :] = part

    own_ref[...] = extra[:length, :]
    for entry, ref in zip(sets, send_refs):
        offset = entry["offset"]
        first = (me // offset) % 2 == entry["colour"]
        side = jnp.where(first, 1, 0)
        if entry["full"]:
            to_low = acc[0, slot_rows(offset), :]
            to_up = acc[1, slot_rows(offset), :]
            more = extra[slot_rows(offset), :]
            ref[:length, :] = jnp.where(first, more, to_low).astype(jnp.bfloat16)
            ref[length:, :] = jnp.where(first, to_up, 0.0).astype(jnp.bfloat16)
        else:
            part = acc[side, slot_rows(offset), :]
            for pair in entry["folds"]:
                part = jnp.where(me == pair[0], extra[slot_rows(pair[1] - pair[0]), :], part)
            ref[...] = part.astype(jnp.bfloat16)


def output_kernel(pb, dsb, kv_win, q_all, g_all, att_hbm, dq_hbm, own_ref, att, dq, sems):
    length = att.shape[0] // 2
    width = HEAD_DIM
    heads = att.shape[1] // width
    scaling = width ** (-0.5)
    group = next(g for g in (4, 2) if heads % g == 0)
    half = length // 2
    tri_row = lax.broadcasted_iota(jnp.int32, (length, 2 * half), 0)
    tri_col = lax.broadcasted_iota(jnp.int32, (length, 2 * half), 1) % half
    copies = []
    for s in range(2):
        k_turn = kv_win[s, :, :width].T
        v_turn = kv_win[s, :, width:].T
        own_weights, own_scores = [], []
        for u in range(2):
            near_low = jnp.where(tri_row <= tri_col + u * half, 1.0, 0.0).astype(jnp.bfloat16)
            for h in range(0, heads, group):
                blocks = [(u * heads + h + j) // 2 for j in range(0, group, 2)]
                weights = [unfolded(pb, s, block, near_low) for block in blocks]
                d_scores = [unfolded(dsb, s, block, near_low) for block in blocks]
                own_weights += [value[:length, :] for value in weights]
                own_scores += [value[:length, :] for value in d_scores]
                out_t = jnp.dot(
                    v_turn, jnp.concatenate(weights, axis=1), preferred_element_type=jnp.float32
                )
                dq_t = jnp.dot(
                    k_turn, jnp.concatenate(d_scores, axis=1), preferred_element_type=jnp.float32
                )
                out_t = out_t.astype(jnp.bfloat16)
                dq_t = (dq_t * scaling).astype(jnp.bfloat16)
                rows = slice((2 * s + u) * half, (2 * s + u + 1) * half)
                for j in range(0, group, 2):
                    part = slice(j * half, (j + 2) * half)
                    for ref, value in ((att, out_t[:, part].T), (dq, dq_t[:, part].T)):
                        for i in range(2):
                            cols = slice((h + j + i) * width, (h + j + i + 1) * width)
                            ref[rows, cols] = value[i * half : (i + 1) * half, :]
        rows = slice(s * length, (s + 1) * length)
        for a, (src, dst) in enumerate(((att, att_hbm), (dq, dq_hbm))):
            copy = pltpu.make_async_copy(src.at[rows, :], dst.at[rows, :], sems.at[s, a])
            copy.start()
            copies.append(copy)
        d_k = jnp.dot(
            jnp.concatenate(own_scores, axis=1),
            jnp.concatenate([stacked(q_all, s, u) for u in range(2)], axis=0),
            preferred_element_type=jnp.float32,
        )
        d_v = jnp.dot(
            jnp.concatenate(own_weights, axis=1),
            jnp.concatenate([stacked(g_all, s, u) for u in range(2)], axis=0),
            preferred_element_type=jnp.float32,
        )
        own_ref[rows, :width] = d_k * scaling
        own_ref[rows, width:] = d_v
    for copy in copies:
        copy.wait()


def sum_kernel(sets, ctx_count, own_ref, fold_ref, *refs):
    dk_ref, dv_ref = refs[len(sets) :]
    me = lax.axis_index("ctx")
    length = own_ref.shape[0] // 2
    width = dk_ref.shape[1]
    low = own_ref[:length, :] + fold_ref[...]
    up = own_ref[length:, :]
    for entry, ref in zip(sets, refs):
        offset = entry["offset"]
        first = (me // offset) % 2 == entry["colour"]
        as_first = first & (me + offset < ctx_count)
        as_second = jnp.logical_not(first) & (me >= offset)
        if entry["full"]:
            low = low + jnp.where(as_first | as_second, ref[:length, :].astype(jnp.float32), 0.0)
            up = up + jnp.where(as_second, ref[length:, :].astype(jnp.float32), 0.0)
        else:
            part = ref[...].astype(jnp.float32)
            for pair in entry["folds"]:
                as_first = as_first & (me != pair[0]) | (me == pair[1])
            low = low + jnp.where(as_first, part, 0.0)
            up = up + jnp.where(as_second, part, 0.0)
    dk_ref[:length, :] = low[:, :width].astype(jnp.bfloat16)
    dk_ref[length:, :] = up[:, :width].astype(jnp.bfloat16)
    dv_ref[:length, :] = low[:, width:].astype(jnp.bfloat16)
    dv_ref[length:, :] = up[:, width:].astype(jnp.bfloat16)


def in_vmem(amount):
    return [pl.BlockSpec(memory_space=pltpu.VMEM)] * amount


def in_place(amount):
    return [pl.BlockSpec(memory_space=pl.ANY)] * amount


def on_chip(values):
    return [pltpu.with_memory_space_constraint(v, pltpu.VMEM) for v in values]


def off_chip(values):
    return [pltpu.with_memory_space_constraint(v, pltpu.HBM) for v in values]


def shards(query_rows, key_rows, value_rows, out_grad, doc_lengths):
    ctx_count = lax.axis_size("ctx")
    head_count = lax.axis_size("head")
    tok_dev = query_rows.shape[0]
    length = tok_dev // 2
    width = key_rows.shape[1]
    reach = min(DOC_STRETCHES, ctx_count // 4)
    span = (reach + 1) * length
    heads = query_rows.shape[1] // width
    sets = exchanges(ctx_count, reach)
    fulls = sum(s["full"] for s in sets)
    count = len(sets)
    payloads = [
        pltpu.VMEM((2 * length if s["full"] else length, 2 * width), jnp.bfloat16) for s in sets
    ]
    mine, *halves = pl.pallas_call(
        lambda *refs: pack_kernel(sets, *refs),
        out_shape=[pltpu.VMEM((tok_dev, 2 * width), jnp.bfloat16)] + payloads[fulls:],
        in_specs=in_place(2),
        out_specs=in_vmem(1 + count - fulls),
        scratch_shapes=[pltpu.SemaphoreType.DMA((2 + 2 * (count - fulls),))],
        compiler_params=pltpu.CompilerParams(vmem_limit_bytes=VMEM_LIMIT),
        name="pack",
    )(*off_chip([key_rows, value_rows]))
    packed = [mine] * fulls + halves
    received = [swap(p, s, ctx_count, head_count, "fetch") for p, s in zip(packed, sets)]

    stack = pltpu.VMEM((heads, tok_dev, width), jnp.bfloat16)
    q_all, g_all, bias = pl.pallas_call(
        lambda *refs: stage_kernel(ctx_count, *refs),
        out_shape=[stack, stack, pltpu.VMEM((2, 2, reach * length, length), jnp.float32)],
        in_specs=in_place(3),
        out_specs=in_vmem(3),
        scratch_shapes=[
            pltpu.SMEM(doc_lengths.shape, jnp.int32),
            pltpu.SemaphoreType.DMA((3, heads)),
        ],
        compiler_params=pltpu.CompilerParams(vmem_limit_bytes=VMEM_LIMIT),
        name="stage",
    )(*off_chip([doc_lengths, query_rows, out_grad]))

    low_weights = pltpu.VMEM((2, heads, reach * length, length), jnp.bfloat16)
    pb, dsb, kv_win, folded, *partials = pl.pallas_call(
        lambda *refs: score_kernel(sets, ctx_count, reach, *refs),
        out_shape=[
            low_weights,
            low_weights,
            pltpu.VMEM((2, span, 2 * width), jnp.bfloat16),
            pltpu.VMEM((length, 2 * width), jnp.float32),
        ]
        + payloads,
        in_specs=in_vmem(4 + count),
        out_specs=in_vmem(4 + count),
        scratch_shapes=[
            pltpu.VMEM((2, span, 2 * width), jnp.float32),
            pltpu.VMEM((reach * length, 2 * width), jnp.float32),
        ],
        compiler_params=pltpu.CompilerParams(vmem_limit_bytes=VMEM_LIMIT),
        name="score",
    )(*on_chip([bias, q_all, g_all, mine, *received]))
    returned = [swap(p, s, ctx_count, head_count, "give") for p, s in zip(partials, sets)]

    attended, query_grad, own = pl.pallas_call(
        output_kernel,
        out_shape=[jax.ShapeDtypeStruct(query_rows.shape, jnp.bfloat16)] * 2
        + [pltpu.VMEM((tok_dev, 2 * width), jnp.float32)],
        in_specs=in_vmem(5),
        out_specs=in_place(2) + in_vmem(1),
        scratch_shapes=[
            pltpu.VMEM(query_rows.shape, jnp.bfloat16),
            pltpu.VMEM(query_rows.shape, jnp.bfloat16),
            pltpu.SemaphoreType.DMA((2, 2)),
        ],
        compiler_params=pltpu.CompilerParams(vmem_limit_bytes=VMEM_LIMIT),
        name="output",
    )(*on_chip([pb, dsb, kv_win, q_all, g_all]))

    key_grad, value_grad = pl.pallas_call(
        lambda *refs: sum_kernel(sets, ctx_count, *refs),
        out_shape=[jax.ShapeDtypeStruct(key_rows.shape, jnp.bfloat16)] * 2,
        in_specs=in_vmem(2 + count),
        out_specs=in_vmem(2),
        compiler_params=pltpu.CompilerParams(vmem_limit_bytes=VMEM_LIMIT),
        name="total",
    )(*on_chip([own, folded, *returned]))
    return (attended, query_grad, key_grad, value_grad)


def solution(mesh):
    placed = (
        P(("groups", "ctx"), "head"),
        P(("groups", "ctx"), "head"),
        P(("groups", "ctx"), "head"),
        P(("groups", "ctx"), "head"),
        P("groups"),
    )
    return jax.shard_map(
        shards,
        mesh=mesh,
        in_specs=placed,
        out_specs=(P(("groups", "ctx"), "head"),) * 4,
        check_vma=False,
    )
```

```python
import math

import jax
import jax.numpy as jnp
from jax import lax
from jax.experimental import pallas as pl
from jax.experimental.pallas import tpu as pltpu
from jax.sharding import PartitionSpec as P


HEAD_DIM = 128
DOC_STRETCHES = 8
MASKED = -1e30
VMEM_LIMIT = 24 << 20


def exchanges(ctx_count, reach):
    sets = []
    for offset in range(1, reach + 1):
        for colour in range(2):
            firsts = [b for b in range(ctx_count - offset) if (b // offset) % 2 == colour]
            if firsts:
                sets.append(dict(offset=offset, colour=colour, full=False, firsts=firsts, folds=[]))
    while not place_folds(sets, ctx_count, reach):
        pass
    return sorted(sets, key=lambda entry: not entry["full"])


def place_folds(sets, ctx_count, reach):
    for entry in sets:
        entry["folds"] = []
    for entry in sets:
        offset = entry["offset"]
        for b in entry["firsts"]:
            if entry["full"] or 2 * b < 2 * ctx_count - 1 - reach - offset:
                continue
            for other in sets:
                busy = [x for f in other["firsts"] for x in (f, f + other["offset"])]
                busy += [x for pair in other["folds"] for x in pair]
                sends_low = ((b + offset) // other["offset"]) % 2 == other["colour"]
                if b not in busy and b + offset not in busy and sends_low and not other["full"]:
                    other["folds"].append((b, b + offset))
                    break
            else:
                entry["full"] = True
                return False
    return True


def key_of(entry):
    return entry["offset"], entry["colour"]


def swap(value, exchange, ctx_count, head_count):
    partner = {}
    pairs = [(b, b + exchange["offset"]) for b in exchange["firsts"]] + exchange["folds"]
    for a, b in pairs:
        partner[a], partner[b] = b, a
    pairs = []
    for b in range(ctx_count):
        for h in range(head_count):
            if b in partner:
                pairs.append((b * head_count + h, partner[b] * head_count + h))
            else:
                pairs.append((b * head_count + h, b * head_count + (h + 1) % head_count))
    return lax.ppermute(value, ("ctx", "head"), pairs)


def fold_offsets(slot):
    return range(-(slot - 1), slot, 2)


def pack_kernel(sets, k_hbm, v_hbm, mine, *refs):
    halves = [s for s in sets if not s["full"]]
    outs, sems = refs[: len(halves)], refs[len(halves)]
    me = lax.axis_index("ctx")
    length = k_hbm.shape[0] // 2
    width = k_hbm.shape[1]
    copies = [
        pltpu.make_async_copy(k_hbm, mine.at[:, :width], sems.at[0]),
        pltpu.make_async_copy(v_hbm, mine.at[:, width:], sems.at[1]),
    ]
    for i, (entry, out) in enumerate(zip(halves, outs)):
        first = (me // entry["offset"]) % 2 == entry["colour"]
        rows = pl.ds(pl.multiple_of(jnp.where(first, 0, length), length), length)
        copies.append(pltpu.make_async_copy(k_hbm.at[rows, :], out.at[:, :width], sems.at[2 * i + 2]))
        copies.append(pltpu.make_async_copy(v_hbm.at[rows, :], out.at[:, width:], sems.at[2 * i + 3]))
    for copy in copies:
        copy.start()
    for copy in copies:
        copy.wait()


def stage_kernel(ctx_count, docs_hbm, q_hbm, g_hbm, q_all, g_all, bias, docs_ref, sems):
    length = q_hbm.shape[0] // 2
    heads, _, width = q_all.shape
    lengths = pltpu.make_async_copy(docs_hbm, docs_ref, sems.at[2, 0])
    lengths.start()
    copies = []
    for h in range(heads):
        cols = slice(h * width, (h + 1) * width)
        for a, (src, dst) in enumerate(((q_hbm, q_all), (g_hbm, g_all))):
            copies.append(pltpu.make_async_copy(src.at[:, cols], dst.at[h], sems.at[a, h]))
    for copy in copies:
        copy.start()
    lengths.wait()
    me = lax.axis_index("ctx")
    merged = bias.shape[2]
    row = lax.broadcasted_iota(jnp.int32, (merged, length), 0)
    half = length // 2
    col = lax.broadcasted_iota(jnp.int32, (1, length), 1) % half
    for s, u in ((0, 0), (0, 1), (1, 0), (1, 1)):
        stretch = me if s == 0 else 2 * ctx_count - 1 - me
        q_pos = stretch * length + u * half + col
        start = jnp.int32(0)
        doc_start = jnp.zeros((1, length), jnp.int32)
        for i in range(docs_ref.shape[0]):
            doc_start = jnp.where(q_pos >= start, start, doc_start)
            start = start + docs_ref[i]
        k_pos = row + (stretch - 2 * (row // length)) * length
        k_pos = jnp.where(k_pos > q_pos, k_pos - merged, k_pos)
        bias[s, u] = jnp.where(k_pos >= doc_start, 0.0, MASKED)
    for copy in copies:
        copy.wait()


def stacked(ref, s, u, first=0, last=None):
    half = ref.shape[1] // 4
    start = (2 * s + u) * half
    return ref[first:last, start : start + half, :].reshape(-1, ref.shape[2])


def unfolded(ref, s, h, near_low):
    length = ref.shape[3]
    value = ref[s, h]
    own = value[:length, :] * near_low
    return jnp.concatenate([own, value[length:, :], value[:length, :] - own], axis=0)


def score_kernel(sets, ctx_count, reach, bias, q_all, g_all, mine, *refs):
    count = len(sets)
    recs = {key_of(s): (r, s["full"]) for s, r in zip(sets, refs[:count])}
    pb, dsb, kv_win, own_ref = refs[count : count + 4]
    send_refs = refs[count + 4 : 2 * count + 4]
    acc, extra = refs[2 * count + 4 :]
    me = lax.axis_index("ctx")
    length = mine.shape[0] // 2
    width = HEAD_DIM
    heads = q_all.shape[0]
    merged = reach * length
    scaling = width ** (-0.5)
    log_scale = scaling * math.log2(math.e)

    def low_part(key):
        ref, full = recs[key]
        return ref[:length, :] if full else ref[...]

    def up_part(key):
        ref, full = recs[key]
        return ref[length:, :] if full else ref[...]

    def pick(part, offset, colour_pred):
        have = [c for c in range(2) if (offset, c) in recs]
        if len(have) == 1:
            return part((offset, have[0]))
        return jnp.where(colour_pred, part((offset, 1)), part((offset, 0)))

    lows = [mine[:length, :]]
    highs = [mine[length:, :]]
    for slot in range(1, reach + 1):
        odd = (me // slot) % 2 == 1
        lows.append(pick(low_part, slot, jnp.logical_not(odd)))
        highs.append(pick(up_part, slot, odd))
    for slot in range(1, reach + 1):
        folded = me + slot >= ctx_count
        value = highs[slot]
        for offset in fold_offsets(slot):
            here = folded & (2 * ctx_count - 1 - 2 * me - slot == offset)
            if offset <= 0:
                value = jnp.where(here, lows[-offset], value)
            else:
                for colour in range(2):
                    if recs.get((offset, colour), (None, False))[1]:
                        where = here & ((me // offset) % 2 == colour)
                        value = jnp.where(where, low_part((offset, colour)), value)
                for entry in sets:
                    for pair in entry["folds"]:
                        if pair[1] - pair[0] == offset:
                            where = here & (me == pair[0])
                            value = jnp.where(where, recs[key_of(entry)][0][...], value)
        highs[slot] = value
    for slot in range(reach + 1):
        rows = slice(slot * length, (slot + 1) * length)
        kv_win[0, rows, :] = lows[slot]
        kv_win[1, rows, :] = highs[slot]

    half = length // 2
    group = next(g for g in (4, 2) if heads % g == 0)
    lanes = 2 * half
    tri_row = lax.broadcasted_iota(jnp.int32, (half, lanes), 0)
    near = tri_row <= lax.broadcasted_iota(jnp.int32, (half, lanes), 1) % half
    far_low = jnp.where(near, 0.0, 1.0).astype(jnp.bfloat16)
    contract_last = (((1,), (1,)), ((), ()))

    def products(s, u, h):
        own_rows = slice(0, length if u else half)
        last_rows = slice(merged + half if u else merged, None)

        def window(cols):
            parts = [kv_win[s, own_rows, cols], kv_win[s, length:merged, cols]]
            return jnp.concatenate(parts + [kv_win[s, last_rows, cols]], axis=0)

        raw = lax.dot_general(
            window(slice(0, width)),
            stacked(q_all, s, u, h, h + group),
            contract_last,
            preferred_element_type=jnp.float32,
        )
        d_p = lax.dot_general(
            window(slice(width, None)),
            stacked(g_all, s, u, h, h + group),
            contract_last,
            preferred_element_type=jnp.float32,
        )
        return raw, d_p

    def fold(u, value):
        if u:
            top = value[:half, :]
            low = jnp.where(near, value[half:length, :], value[merged:, :])
            middle = value[length:merged, :]
        else:
            last = value[merged - half :, :]
            top = jnp.where(near, value[:half, :], last[:half, :])
            low = last[half:, :]
            middle = value[half : merged - half, :]
        return jnp.concatenate([top, low, middle], axis=0)

    def soften(s, u, block, raw, d_p):
        raw = fold(u, raw) + bias[s, u]
        d_p = fold(u, d_p)
        top = jnp.max(raw, axis=0, keepdims=True)
        weight = jnp.exp2((raw - top) * log_scale)
        total = jnp.sum(weight, axis=0, keepdims=True)
        inverse = 1.0 / total
        delta = jnp.sum(weight * d_p, axis=0, keepdims=True) * inverse
        weight = weight * inverse
        others = []
        for ref, value in ((pb, weight), (dsb, weight * (d_p - delta))):
            value = value.astype(jnp.bfloat16)
            ref[s, block] = value
            if u:
                last = [value[half:length, :] * far_low]
            else:
                last = [value[:half, :] * far_low, value[half:length, :]]
            others.append(jnp.concatenate([value[length:, :]] + last, axis=0))
        return others

    def gradients(s, u, first, last, start, done):
        weights, d_scores = [jnp.concatenate(values, axis=1) for values in zip(*done)]
        parts = [(slice(length, merged), slice(0, merged - length))] if merged > length else []
        parts.append((slice(merged + u * half, merged + length), slice(merged - length, None)))
        for cols, left, right in (
            (slice(0, width), d_scores, q_all),
            (slice(width, None), weights, g_all),
        ):
            value = jnp.dot(
                left, stacked(right, s, u, first, last), preferred_element_type=jnp.float32
            )
            if right is q_all:
                value = value * scaling
            for rows, part in parts:
                if start:
                    acc[s, rows, cols] = value[part, :]
                else:
                    acc[s, rows, cols] = acc[s, rows, cols] + value[part, :]

    items = [(s, u, h) for s in range(2) for u in range(2) for h in range(0, heads, group)]
    done = []
    ready = products(*items[0])
    for i, (s, u, h) in enumerate(items):
        following = products(*items[i + 1]) if i + 1 < len(items) else None
        for j in range(0, group, 2):
            part = slice(j // 2 * lanes, (j // 2 + 1) * lanes)
            block = (u * heads + h + j) // 2
            done.append(soften(s, u, block, ready[0][:, part], ready[1][:, part]))
        ready = following
        last = h + group
        if last == heads or (s, u) == (1, 1) and last == heads - group:
            first = last - 2 * len(done)
            gradients(s, u, first, last, u == 0, done)
            done = []

    def slot_rows(slot):
        return slice(slot * length, (slot + 1) * length)

    extra[...] = jnp.zeros(extra.shape, jnp.float32)
    for slot in range(1, reach + 1):
        for offset in fold_offsets(slot):

            @pl.when((me + slot >= ctx_count) & (2 * ctx_count - 1 - 2 * me - slot == offset))
            def _():
                part = acc[1, slot_rows(slot), :]
                if offset < 0:
                    acc[0, slot_rows(-offset), :] = acc[0, slot_rows(-offset), :] + part
                else:
                    extra[slot_rows(offset), :] = part

    own_ref[...] = extra[:length, :]
    for entry, ref in zip(sets, send_refs):
        offset = entry["offset"]
        first = (me // offset) % 2 == entry["colour"]
        side = jnp.where(first, 1, 0)
        if entry["full"]:
            to_low = acc[0, slot_rows(offset), :]
            to_up = acc[1, slot_rows(offset), :]
            more = extra[slot_rows(offset), :]
            ref[:length, :] = jnp.where(first, more, to_low).astype(jnp.bfloat16)
            ref[length:, :] = jnp.where(first, to_up, 0.0).astype(jnp.bfloat16)
        else:
            part = acc[side, slot_rows(offset), :]
            for pair in entry["folds"]:
                part = jnp.where(me == pair[0], extra[slot_rows(pair[1] - pair[0]), :], part)
            ref[...] = part.astype(jnp.bfloat16)


def output_kernel(pb, dsb, kv_win, q_all, g_all, att_hbm, dq_hbm, own_ref, att, dq, sems):
    length = att.shape[0] // 2
    width = HEAD_DIM
    heads = att.shape[1] // width
    scaling = width ** (-0.5)
    group = next(g for g in (4, 2) if heads % g == 0)
    half = length // 2
    tri_row = lax.broadcasted_iota(jnp.int32, (length, 2 * half), 0)
    tri_col = lax.broadcasted_iota(jnp.int32, (length, 2 * half), 1) % half
    copies = []
    for s in range(2):
        k_turn = kv_win[s, :, :width].T
        v_turn = kv_win[s, :, width:].T
        own_weights, own_scores = [], []
        for u in range(2):
            near_low = jnp.where(tri_row <= tri_col + u * half, 1.0, 0.0).astype(jnp.bfloat16)
            for h in range(0, heads, group):
                blocks = [(u * heads + h + j) // 2 for j in range(0, group, 2)]
                weights = [unfolded(pb, s, block, near_low) for block in blocks]
                d_scores = [unfolded(dsb, s, block, near_low) for block in blocks]
                own_weights += [value[:length, :] for value in weights]
                own_scores += [value[:length, :] for value in d_scores]
                out_t = jnp.dot(
                    v_turn, jnp.concatenate(weights, axis=1), preferred_element_type=jnp.float32
                )
                dq_t = jnp.dot(
                    k_turn, jnp.concatenate(d_scores, axis=1), preferred_element_type=jnp.float32
                )
                out_t = out_t.astype(jnp.bfloat16)
                dq_t = (dq_t * scaling).astype(jnp.bfloat16)
                rows = slice((2 * s + u) * half, (2 * s + u + 1) * half)
                for j in range(0, group, 2):
                    part = slice(j * half, (j + 2) * half)
                    for ref, value in ((att, out_t[:, part].T), (dq, dq_t[:, part].T)):
                        for i in range(2):
                            cols = slice((h + j + i) * width, (h + j + i + 1) * width)
                            ref[rows, cols] = value[i * half : (i + 1) * half, :]
        rows = slice(s * length, (s + 1) * length)
        for a, (src, dst) in enumerate(((att, att_hbm), (dq, dq_hbm))):
            copy = pltpu.make_async_copy(src.at[rows, :], dst.at[rows, :], sems.at[s, a])
            copy.start()
            copies.append(copy)
        d_k = jnp.dot(
            jnp.concatenate(own_scores, axis=1),
            jnp.concatenate([stacked(q_all, s, u) for u in range(2)], axis=0),
            preferred_element_type=jnp.float32,
        )
        d_v = jnp.dot(
            jnp.concatenate(own_weights, axis=1),
            jnp.concatenate([stacked(g_all, s, u) for u in range(2)], axis=0),
            preferred_element_type=jnp.float32,
        )
        own_ref[rows, :width] = d_k * scaling
        own_ref[rows, width:] = d_v
    for copy in copies:
        copy.wait()


def sum_kernel(sets, ctx_count, own_ref, fold_ref, *refs):
    dk_ref, dv_ref = refs[len(sets) :]
    me = lax.axis_index("ctx")
    length = own_ref.shape[0] // 2
    width = dk_ref.shape[1]
    low = own_ref[:length, :] + fold_ref[...]
    up = own_ref[length:, :]
    for entry, ref in zip(sets, refs):
        offset = entry["offset"]
        first = (me // offset) % 2 == entry["colour"]
        as_first = first & (me + offset < ctx_count)
        as_second = jnp.logical_not(first) & (me >= offset)
        if entry["full"]:
            low = low + jnp.where(as_first | as_second, ref[:length, :].astype(jnp.float32), 0.0)
            up = up + jnp.where(as_second, ref[length:, :].astype(jnp.float32), 0.0)
        else:
            part = ref[...].astype(jnp.float32)
            for pair in entry["folds"]:
                as_first = as_first & (me != pair[0]) | (me == pair[1])
            low = low + jnp.where(as_first, part, 0.0)
            up = up + jnp.where(as_second, part, 0.0)
    dk_ref[:length, :] = low[:, :width].astype(jnp.bfloat16)
    dk_ref[length:, :] = up[:, :width].astype(jnp.bfloat16)
    dv_ref[:length, :] = low[:, width:].astype(jnp.bfloat16)
    dv_ref[length:, :] = up[:, width:].astype(jnp.bfloat16)


def in_vmem(amount):
    return [pl.BlockSpec(memory_space=pltpu.VMEM)] * amount


def in_place(amount):
    return [pl.BlockSpec(memory_space=pl.ANY)] * amount


def on_chip(values):
    return [pltpu.with_memory_space_constraint(v, pltpu.VMEM) for v in values]


def off_chip(values):
    return [pltpu.with_memory_space_constraint(v, pltpu.HBM) for v in values]


def attention(query_rows, key_rows, value_rows, out_grad, doc_lengths):
    ctx_count = lax.axis_size("ctx")
    head_count = lax.axis_size("head")
    tok_dev = query_rows.shape[0]
    length = tok_dev // 2
    width = key_rows.shape[1]
    reach = min(DOC_STRETCHES, ctx_count // 4)
    span = (reach + 1) * length
    heads = query_rows.shape[1] // width
    sets = exchanges(ctx_count, reach)
    fulls = sum(s["full"] for s in sets)
    count = len(sets)
    payloads = [
        pltpu.VMEM((2 * length if s["full"] else length, 2 * width), jnp.bfloat16) for s in sets
    ]
    mine, *halves = pl.pallas_call(
        lambda *refs: pack_kernel(sets, *refs),
        out_shape=[pltpu.VMEM((tok_dev, 2 * width), jnp.bfloat16)] + payloads[fulls:],
        in_specs=in_place(2),
        out_specs=in_vmem(1 + count - fulls),
        scratch_shapes=[pltpu.SemaphoreType.DMA((2 + 2 * (count - fulls),))],
        compiler_params=pltpu.CompilerParams(vmem_limit_bytes=VMEM_LIMIT),
        name="pack",
    )(*off_chip([key_rows, value_rows]))
    packed = [mine] * fulls + halves
    received = [swap(p, s, ctx_count, head_count) for p, s in zip(packed, sets)]

    stack = pltpu.VMEM((heads, tok_dev, width), jnp.bfloat16)
    q_all, g_all, bias = pl.pallas_call(
        lambda *refs: stage_kernel(ctx_count, *refs),
        out_shape=[stack, stack, pltpu.VMEM((2, 2, reach * length, length), jnp.float32)],
        in_specs=in_place(3),
        out_specs=in_vmem(3),
        scratch_shapes=[
            pltpu.SMEM(doc_lengths.shape, jnp.int32),
            pltpu.SemaphoreType.DMA((3, heads)),
        ],
        compiler_params=pltpu.CompilerParams(vmem_limit_bytes=VMEM_LIMIT),
        name="stage",
    )(*off_chip([doc_lengths, query_rows, out_grad]))

    low_weights = pltpu.VMEM((2, heads, reach * length, length), jnp.bfloat16)
    pb, dsb, kv_win, folded, *partials = pl.pallas_call(
        lambda *refs: score_kernel(sets, ctx_count, reach, *refs),
        out_shape=[
            low_weights,
            low_weights,
            pltpu.VMEM((2, span, 2 * width), jnp.bfloat16),
            pltpu.VMEM((length, 2 * width), jnp.float32),
        ]
        + payloads,
        in_specs=in_vmem(4 + count),
        out_specs=in_vmem(4 + count),
        scratch_shapes=[
            pltpu.VMEM((2, span, 2 * width), jnp.float32),
            pltpu.VMEM((reach * length, 2 * width), jnp.float32),
        ],
        compiler_params=pltpu.CompilerParams(vmem_limit_bytes=VMEM_LIMIT),
        name="score",
    )(*on_chip([bias, q_all, g_all, mine, *received]))
    returned = [swap(p, s, ctx_count, head_count) for p, s in zip(partials, sets)]

    attended, query_grad, own = pl.pallas_call(
        output_kernel,
        out_shape=[jax.ShapeDtypeStruct(query_rows.shape, jnp.bfloat16)] * 2
        + [pltpu.VMEM((tok_dev, 2 * width), jnp.float32)],
        in_specs=in_vmem(5),
        out_specs=in_place(2) + in_vmem(1),
        scratch_shapes=[
            pltpu.VMEM(query_rows.shape, jnp.bfloat16),
            pltpu.VMEM(query_rows.shape, jnp.bfloat16),
            pltpu.SemaphoreType.DMA((2, 2)),
        ],
        compiler_params=pltpu.CompilerParams(vmem_limit_bytes=VMEM_LIMIT),
        name="output",
    )(*on_chip([pb, dsb, kv_win, q_all, g_all]))

    key_grad, value_grad = pl.pallas_call(
        lambda *refs: sum_kernel(sets, ctx_count, *refs),
        out_shape=[jax.ShapeDtypeStruct(key_rows.shape, jnp.bfloat16)] * 2,
        in_specs=in_vmem(2 + count),
        out_specs=in_vmem(2),
        compiler_params=pltpu.CompilerParams(vmem_limit_bytes=VMEM_LIMIT),
        name="total",
    )(*on_chip([own, folded, *returned]))
    return (attended, query_grad, key_grad, value_grad)


def solution(mesh):
    placed = (
        P(("groups", "ctx"), "head"),
        P(("groups", "ctx"), "head"),
        P(("groups", "ctx"), "head"),
        P(("groups", "ctx"), "head"),
        P("groups"),
    )
    return jax.shard_map(
        attention,
        mesh=mesh,
        in_specs=placed,
        out_specs=(P(("groups", "ctx"), "head"),) * 4,
        check_vma=False,
    )
```

```python
import math

import jax
import jax.numpy as jnp
from jax import lax
from jax.experimental import pallas as pl
from jax.experimental.pallas import tpu as pltpu
from jax.sharding import PartitionSpec as P


HEAD_DIM = 128
DOC_STRETCHES = 8
MASKED = -1e30
VMEM_LIMIT = 24 << 20


def exchanges(ctx_count, reach):
    sets = []
    for offset in range(1, reach + 1):
        for colour in range(2):
            firsts = [b for b in range(ctx_count - offset) if (b // offset) % 2 == colour]
            if firsts:
                sets.append(dict(offset=offset, colour=colour, full=False, firsts=firsts, folds=[]))
    while not place_folds(sets, ctx_count, reach):
        pass
    return sorted(sets, key=lambda entry: not entry["full"])


def place_folds(sets, ctx_count, reach):
    for entry in sets:
        entry["folds"] = []
    for entry in sets:
        offset = entry["offset"]
        for b in entry["firsts"]:
            if entry["full"] or 2 * b < 2 * ctx_count - 1 - reach - offset:
                continue
            for other in sets:
                busy = [x for f in other["firsts"] for x in (f, f + other["offset"])]
                busy += [x for pair in other["folds"] for x in pair]
                sends_low = ((b + offset) // other["offset"]) % 2 == other["colour"]
                if b not in busy and b + offset not in busy and sends_low and not other["full"]:
                    other["folds"].append((b, b + offset))
                    break
            else:
                entry["full"] = True
                return False
    return True


def key_of(entry):
    return entry["offset"], entry["colour"]


def swap(value, exchange, ctx_count, head_count):
    partner = {}
    pairs = [(b, b + exchange["offset"]) for b in exchange["firsts"]] + exchange["folds"]
    for a, b in pairs:
        partner[a], partner[b] = b, a
    pairs = []
    for b in range(ctx_count):
        for h in range(head_count):
            if b in partner:
                pairs.append((b * head_count + h, partner[b] * head_count + h))
            else:
                pairs.append((b * head_count + h, b * head_count + (h + 1) % head_count))
    return lax.ppermute(value, ("ctx", "head"), pairs)


def fold_offsets(slot):
    return range(-(slot - 1), slot, 2)


def pack_kernel(sets, k_hbm, v_hbm, *refs):
    outs, sems = refs[: len(sets)], refs[len(sets)]
    me = lax.axis_index("ctx")
    length = k_hbm.shape[0] // 2
    width = k_hbm.shape[1]
    copies = []
    for i, (entry, out) in enumerate(zip(sets, outs)):
        first = (me // entry["offset"]) % 2 == entry["colour"]
        rows = pl.ds(pl.multiple_of(jnp.where(first, 0, length), length), length)
        for a, hbm in enumerate((k_hbm, v_hbm)):
            src = hbm if entry["full"] else hbm.at[rows, :]
            cols = slice(a * width, (a + 1) * width)
            copies.append(pltpu.make_async_copy(src, out.at[:, cols], sems.at[i, a]))
    for copy in copies:
        copy.start()
    for copy in copies:
        copy.wait()


def stage_kernel(
    ctx_count, docs_hbm, q_hbm, g_hbm, k_hbm, v_hbm, q_all, g_all, mine, bias, docs_ref, sems
):
    length = q_hbm.shape[0] // 2
    heads, _, width = q_all.shape
    lengths = pltpu.make_async_copy(docs_hbm, docs_ref, sems.at[2, 0])
    lengths.start()
    copies = [
        pltpu.make_async_copy(k_hbm, mine.at[:, :width], sems.at[2, 1]),
        pltpu.make_async_copy(v_hbm, mine.at[:, width:], sems.at[2, 2]),
    ]
    for h in range(heads):
        cols = slice(h * width, (h + 1) * width)
        for a, (src, dst) in enumerate(((q_hbm, q_all), (g_hbm, g_all))):
            copies.append(pltpu.make_async_copy(src.at[:, cols], dst.at[h], sems.at[a, h]))
    for copy in copies:
        copy.start()
    lengths.wait()
    me = lax.axis_index("ctx")
    merged = bias.shape[2]
    row = lax.broadcasted_iota(jnp.int32, (merged, length), 0)
    half = length // 2
    col = lax.broadcasted_iota(jnp.int32, (1, length), 1) % half
    for s, u in ((0, 0), (0, 1), (1, 0), (1, 1)):
        stretch = me if s == 0 else 2 * ctx_count - 1 - me
        q_pos = stretch * length + u * half + col
        start = jnp.int32(0)
        doc_start = jnp.zeros((1, length), jnp.int32)
        for i in range(docs_ref.shape[0]):
            doc_start = jnp.where(q_pos >= start, start, doc_start)
            start = start + docs_ref[i]
        k_pos = row + (stretch - 2 * (row // length)) * length
        k_pos = jnp.where(k_pos > q_pos, k_pos - merged, k_pos)
        bias[s, u] = jnp.where(k_pos >= doc_start, 0.0, MASKED)
    for copy in copies:
        copy.wait()


def stacked(ref, s, u, first=0, last=None):
    half = ref.shape[1] // 4
    start = (2 * s + u) * half
    return ref[first:last, start : start + half, :].reshape(-1, ref.shape[2])


def unfolded(ref, s, h, near_low):
    length = ref.shape[3]
    value = ref[s, h]
    own = value[:length, :] * near_low
    return jnp.concatenate([own, value[length:, :], value[:length, :] - own], axis=0)


def score_kernel(sets, ctx_count, reach, bias, q_all, g_all, mine, *refs):
    count = len(sets)
    recs = {key_of(s): (r, s["full"]) for s, r in zip(sets, refs[:count])}
    pb, dsb, kv_win, own_ref = refs[count : count + 4]
    send_refs = refs[count + 4 : 2 * count + 4]
    acc, extra = refs[2 * count + 4 :]
    me = lax.axis_index("ctx")
    length = mine.shape[0] // 2
    width = HEAD_DIM
    heads = q_all.shape[0]
    merged = reach * length
    scaling = width ** (-0.5)
    log_scale = scaling * math.log2(math.e)

    def low_part(key):
        ref, full = recs[key]
        return ref[:length, :] if full else ref[...]

    def up_part(key):
        ref, full = recs[key]
        return ref[length:, :] if full else ref[...]

    def pick(part, offset, colour_pred):
        have = [c for c in range(2) if (offset, c) in recs]
        if len(have) == 1:
            return part((offset, have[0]))
        return jnp.where(colour_pred, part((offset, 1)), part((offset, 0)))

    lows = [mine[:length, :]]
    highs = [mine[length:, :]]
    for slot in range(1, reach + 1):
        odd = (me // slot) % 2 == 1
        lows.append(pick(low_part, slot, jnp.logical_not(odd)))
        highs.append(pick(up_part, slot, odd))
    for slot in range(1, reach + 1):
        folded = me + slot >= ctx_count
        value = highs[slot]
        for offset in fold_offsets(slot):
            here = folded & (2 * ctx_count - 1 - 2 * me - slot == offset)
            if offset <= 0:
                value = jnp.where(here, lows[-offset], value)
            else:
                for colour in range(2):
                    if recs.get((offset, colour), (None, False))[1]:
                        where = here & ((me // offset) % 2 == colour)
                        value = jnp.where(where, low_part((offset, colour)), value)
                for entry in sets:
                    for pair in entry["folds"]:
                        if pair[1] - pair[0] == offset:
                            where = here & (me == pair[0])
                            value = jnp.where(where, recs[key_of(entry)][0][...], value)
        highs[slot] = value
    for slot in range(reach + 1):
        rows = slice(slot * length, (slot + 1) * length)
        kv_win[0, rows, :] = lows[slot]
        kv_win[1, rows, :] = highs[slot]

    half = length // 2
    group = next(g for g in (4, 2) if heads % g == 0)
    lanes = 2 * half
    tri_row = lax.broadcasted_iota(jnp.int32, (half, lanes), 0)
    near = tri_row <= lax.broadcasted_iota(jnp.int32, (half, lanes), 1) % half
    far_low = jnp.where(near, 0.0, 1.0).astype(jnp.bfloat16)
    contract_last = (((1,), (1,)), ((), ()))

    def products(s, u, h):
        own_rows = slice(0, length if u else half)
        last_rows = slice(merged + half if u else merged, None)

        def window(cols):
            parts = [kv_win[s, own_rows, cols], kv_win[s, length:merged, cols]]
            return jnp.concatenate(parts + [kv_win[s, last_rows, cols]], axis=0)

        raw = lax.dot_general(
            window(slice(0, width)),
            stacked(q_all, s, u, h, h + group),
            contract_last,
            preferred_element_type=jnp.float32,
        )
        d_p = lax.dot_general(
            window(slice(width, None)),
            stacked(g_all, s, u, h, h + group),
            contract_last,
            preferred_element_type=jnp.float32,
        )
        return raw, d_p

    def fold(u, value):
        if u:
            top = value[:half, :]
            low = jnp.where(near, value[half:length, :], value[merged:, :])
            middle = value[length:merged, :]
        else:
            last = value[merged - half :, :]
            top = jnp.where(near, value[:half, :], last[:half, :])
            low = last[half:, :]
            middle = value[half : merged - half, :]
        return jnp.concatenate([top, low, middle], axis=0)

    def soften(s, u, block, raw, d_p):
        raw = fold(u, raw) + bias[s, u]
        d_p = fold(u, d_p)
        top = jnp.max(raw, axis=0, keepdims=True)
        weight = jnp.exp2((raw - top) * log_scale)
        total = jnp.sum(weight, axis=0, keepdims=True)
        inverse = 1.0 / total
        delta = jnp.sum(weight * d_p, axis=0, keepdims=True) * inverse
        weight = weight * inverse
        others = []
        for ref, value in ((pb, weight), (dsb, weight * (d_p - delta))):
            value = value.astype(jnp.bfloat16)
            ref[s, block] = value
            if u:
                last = [value[half:length, :] * far_low]
            else:
                last = [value[:half, :] * far_low, value[half:length, :]]
            others.append(jnp.concatenate([value[length:, :]] + last, axis=0))
        return others

    def gradients(s, u, first, last, start, done):
        weights, d_scores = [jnp.concatenate(values, axis=1) for values in zip(*done)]
        parts = [(slice(length, merged), slice(0, merged - length))] if merged > length else []
        parts.append((slice(merged + u * half, merged + length), slice(merged - length, None)))
        for cols, left, right in (
            (slice(0, width), d_scores, q_all),
            (slice(width, None), weights, g_all),
        ):
            value = jnp.dot(
                left, stacked(right, s, u, first, last), preferred_element_type=jnp.float32
            )
            if right is q_all:
                value = value * scaling
            for rows, part in parts:
                if start:
                    acc[s, rows, cols] = value[part, :]
                else:
                    acc[s, rows, cols] = acc[s, rows, cols] + value[part, :]

    items = [(s, u, h) for s in range(2) for u in range(2) for h in range(0, heads, group)]
    done = []
    ready = products(*items[0])
    for i, (s, u, h) in enumerate(items):
        following = products(*items[i + 1]) if i + 1 < len(items) else None
        for j in range(0, group, 2):
            part = slice(j // 2 * lanes, (j // 2 + 1) * lanes)
            block = (u * heads + h + j) // 2
            done.append(soften(s, u, block, ready[0][:, part], ready[1][:, part]))
        ready = following
        last = h + group
        if last == heads or (s, u) == (1, 1) and last == heads - group:
            first = last - 2 * len(done)
            gradients(s, u, first, last, u == 0, done)
            done = []

    def slot_rows(slot):
        return slice(slot * length, (slot + 1) * length)

    extra[...] = jnp.zeros(extra.shape, jnp.float32)
    for slot in range(1, reach + 1):
        for offset in fold_offsets(slot):

            @pl.when((me + slot >= ctx_count) & (2 * ctx_count - 1 - 2 * me - slot == offset))
            def _():
                part = acc[1, slot_rows(slot), :]
                if offset < 0:
                    acc[0, slot_rows(-offset), :] = acc[0, slot_rows(-offset), :] + part
                else:
                    extra[slot_rows(offset), :] = part

    own_ref[...] = extra[:length, :]
    for entry, ref in zip(sets, send_refs):
        offset = entry["offset"]
        first = (me // offset) % 2 == entry["colour"]
        side = jnp.where(first, 1, 0)
        if entry["full"]:
            to_low = acc[0, slot_rows(offset), :]
            to_up = acc[1, slot_rows(offset), :]
            more = extra[slot_rows(offset), :]
            ref[:length, :] = jnp.where(first, more, to_low).astype(jnp.bfloat16)
            ref[length:, :] = jnp.where(first, to_up, 0.0).astype(jnp.bfloat16)
        else:
            part = acc[side, slot_rows(offset), :]
            for pair in entry["folds"]:
                part = jnp.where(me == pair[0], extra[slot_rows(pair[1] - pair[0]), :], part)
            ref[...] = part.astype(jnp.bfloat16)


def output_kernel(pb, dsb, kv_win, q_all, g_all, att_hbm, dq_hbm, own_ref, att, dq, sems):
    length = att.shape[0] // 2
    width = HEAD_DIM
    heads = att.shape[1] // width
    scaling = width ** (-0.5)
    group = next(g for g in (4, 2) if heads % g == 0)
    half = length // 2
    tri_row = lax.broadcasted_iota(jnp.int32, (length, 2 * half), 0)
    tri_col = lax.broadcasted_iota(jnp.int32, (length, 2 * half), 1) % half
    copies = []
    for s in range(2):
        k_turn = kv_win[s, :, :width].T
        v_turn = kv_win[s, :, width:].T
        own_weights, own_scores = [], []
        for u in range(2):
            near_low = jnp.where(tri_row <= tri_col + u * half, 1.0, 0.0).astype(jnp.bfloat16)
            for h in range(0, heads, group):
                blocks = [(u * heads + h + j) // 2 for j in range(0, group, 2)]
                weights = [unfolded(pb, s, block, near_low) for block in blocks]
                d_scores = [unfolded(dsb, s, block, near_low) for block in blocks]
                own_weights += [value[:length, :] for value in weights]
                own_scores += [value[:length, :] for value in d_scores]
                out_t = jnp.dot(
                    v_turn, jnp.concatenate(weights, axis=1), preferred_element_type=jnp.float32
                )
                dq_t = jnp.dot(
                    k_turn, jnp.concatenate(d_scores, axis=1), preferred_element_type=jnp.float32
                )
                out_t = out_t.astype(jnp.bfloat16)
                dq_t = (dq_t * scaling).astype(jnp.bfloat16)
                rows = slice((2 * s + u) * half, (2 * s + u + 1) * half)
                for j in range(0, group, 2):
                    part = slice(j * half, (j + 2) * half)
                    for ref, value in ((att, out_t[:, part].T), (dq, dq_t[:, part].T)):
                        for i in range(2):
                            cols = slice((h + j + i) * width, (h + j + i + 1) * width)
                            ref[rows, cols] = value[i * half : (i + 1) * half, :]
        rows = slice(s * length, (s + 1) * length)
        for a, (src, dst) in enumerate(((att, att_hbm), (dq, dq_hbm))):
            copy = pltpu.make_async_copy(src.at[rows, :], dst.at[rows, :], sems.at[s, a])
            copy.start()
            copies.append(copy)
        d_k = jnp.dot(
            jnp.concatenate(own_scores, axis=1),
            jnp.concatenate([stacked(q_all, s, u) for u in range(2)], axis=0),
            preferred_element_type=jnp.float32,
        )
        d_v = jnp.dot(
            jnp.concatenate(own_weights, axis=1),
            jnp.concatenate([stacked(g_all, s, u) for u in range(2)], axis=0),
            preferred_element_type=jnp.float32,
        )
        own_ref[rows, :width] = d_k * scaling
        own_ref[rows, width:] = d_v
    for copy in copies:
        copy.wait()


def sum_kernel(sets, ctx_count, own_ref, fold_ref, *refs):
    dk_ref, dv_ref = refs[len(sets) :]
    me = lax.axis_index("ctx")
    length = own_ref.shape[0] // 2
    width = dk_ref.shape[1]
    low = own_ref[:length, :] + fold_ref[...]
    up = own_ref[length:, :]
    for entry, ref in zip(sets, refs):
        offset = entry["offset"]
        first = (me // offset) % 2 == entry["colour"]
        as_first = first & (me + offset < ctx_count)
        as_second = jnp.logical_not(first) & (me >= offset)
        if entry["full"]:
            low = low + jnp.where(as_first | as_second, ref[:length, :].astype(jnp.float32), 0.0)
            up = up + jnp.where(as_second, ref[length:, :].astype(jnp.float32), 0.0)
        else:
            part = ref[...].astype(jnp.float32)
            for pair in entry["folds"]:
                as_first = as_first & (me != pair[0]) | (me == pair[1])
            low = low + jnp.where(as_first, part, 0.0)
            up = up + jnp.where(as_second, part, 0.0)
    dk_ref[:length, :] = low[:, :width].astype(jnp.bfloat16)
    dk_ref[length:, :] = up[:, :width].astype(jnp.bfloat16)
    dv_ref[:length, :] = low[:, width:].astype(jnp.bfloat16)
    dv_ref[length:, :] = up[:, width:].astype(jnp.bfloat16)


def in_vmem(amount):
    return [pl.BlockSpec(memory_space=pltpu.VMEM)] * amount


def in_place(amount):
    return [pl.BlockSpec(memory_space=pl.ANY)] * amount


def on_chip(values):
    return [pltpu.with_memory_space_constraint(v, pltpu.VMEM) for v in values]


def off_chip(values):
    return [pltpu.with_memory_space_constraint(v, pltpu.HBM) for v in values]


def attention(query_rows, key_rows, value_rows, out_grad, doc_lengths):
    ctx_count = lax.axis_size("ctx")
    head_count = lax.axis_size("head")
    tok_dev = query_rows.shape[0]
    length = tok_dev // 2
    width = key_rows.shape[1]
    reach = min(DOC_STRETCHES, ctx_count // 4)
    span = (reach + 1) * length
    heads = query_rows.shape[1] // width
    sets = exchanges(ctx_count, reach)
    count = len(sets)
    payloads = [
        pltpu.VMEM((2 * length if s["full"] else length, 2 * width), jnp.bfloat16) for s in sets
    ]
    keys_values = off_chip([key_rows, value_rows])
    packed = pl.pallas_call(
        lambda *refs: pack_kernel(sets, *refs),
        out_shape=payloads,
        in_specs=in_place(2),
        out_specs=in_vmem(count),
        scratch_shapes=[pltpu.SemaphoreType.DMA((count, 2))],
        compiler_params=pltpu.CompilerParams(vmem_limit_bytes=VMEM_LIMIT),
        name="pack",
    )(*keys_values)
    received = [swap(p, s, ctx_count, head_count) for p, s in zip(packed, sets)]

    stack = pltpu.VMEM((heads, tok_dev, width), jnp.bfloat16)
    q_all, g_all, mine, bias = pl.pallas_call(
        lambda *refs: stage_kernel(ctx_count, *refs),
        out_shape=[
            stack,
            stack,
            pltpu.VMEM((tok_dev, 2 * width), jnp.bfloat16),
            pltpu.VMEM((2, 2, reach * length, length), jnp.float32),
        ],
        in_specs=in_place(5),
        out_specs=in_vmem(4),
        scratch_shapes=[
            pltpu.SMEM(doc_lengths.shape, jnp.int32),
            pltpu.SemaphoreType.DMA((3, heads)),
        ],
        compiler_params=pltpu.CompilerParams(vmem_limit_bytes=VMEM_LIMIT),
        name="stage",
    )(*off_chip([doc_lengths, query_rows, out_grad]), *keys_values)

    low_weights = pltpu.VMEM((2, heads, reach * length, length), jnp.bfloat16)
    pb, dsb, kv_win, folded, *partials = pl.pallas_call(
        lambda *refs: score_kernel(sets, ctx_count, reach, *refs),
        out_shape=[
            low_weights,
            low_weights,
            pltpu.VMEM((2, span, 2 * width), jnp.bfloat16),
            pltpu.VMEM((length, 2 * width), jnp.float32),
        ]
        + payloads,
        in_specs=in_vmem(4 + count),
        out_specs=in_vmem(4 + count),
        scratch_shapes=[
            pltpu.VMEM((2, span, 2 * width), jnp.float32),
            pltpu.VMEM((reach * length, 2 * width), jnp.float32),
        ],
        compiler_params=pltpu.CompilerParams(vmem_limit_bytes=VMEM_LIMIT),
        name="score",
    )(*on_chip([bias, q_all, g_all, mine, *received]))
    returned = [swap(p, s, ctx_count, head_count) for p, s in zip(partials, sets)]

    attended, query_grad, own = pl.pallas_call(
        output_kernel,
        out_shape=[jax.ShapeDtypeStruct(query_rows.shape, jnp.bfloat16)] * 2
        + [pltpu.VMEM((tok_dev, 2 * width), jnp.float32)],
        in_specs=in_vmem(5),
        out_specs=in_place(2) + in_vmem(1),
        scratch_shapes=[
            pltpu.VMEM(query_rows.shape, jnp.bfloat16),
            pltpu.VMEM(query_rows.shape, jnp.bfloat16),
            pltpu.SemaphoreType.DMA((2, 2)),
        ],
        compiler_params=pltpu.CompilerParams(vmem_limit_bytes=VMEM_LIMIT),
        name="output",
    )(*on_chip([pb, dsb, kv_win, q_all, g_all]))

    key_grad, value_grad = pl.pallas_call(
        lambda *refs: sum_kernel(sets, ctx_count, *refs),
        out_shape=[jax.ShapeDtypeStruct(key_rows.shape, jnp.bfloat16)] * 2,
        in_specs=in_vmem(2 + count),
        out_specs=in_vmem(2),
        compiler_params=pltpu.CompilerParams(vmem_limit_bytes=VMEM_LIMIT),
        name="total",
    )(*on_chip([own, folded, *returned]))
    return (attended, query_grad, key_grad, value_grad)


def solution(mesh):
    placed = (
        P(("groups", "ctx"), "head"),
        P(("groups", "ctx"), "head"),
        P(("groups", "ctx"), "head"),
        P(("groups", "ctx"), "head"),
        P("groups"),
    )
    return jax.shard_map(
        attention,
        mesh=mesh,
        in_specs=placed,
        out_specs=(P(("groups", "ctx"), "head"),) * 4,
        check_vma=False,
    )
```

```python
import math

import jax
import jax.numpy as jnp
from jax import lax
from jax.experimental import pallas as pl
from jax.experimental.pallas import tpu as pltpu
from jax.sharding import PartitionSpec as P


HEAD_DIM = 128
DOC_STRETCHES = 8
MASKED = -1e30
VMEM_LIMIT = 24 << 20


def exchanges(ctx_count, reach):
    sets = []
    for offset in range(1, reach + 1):
        for colour in range(2):
            firsts = [b for b in range(ctx_count - offset) if (b // offset) % 2 == colour]
            if firsts:
                sets.append(dict(offset=offset, colour=colour, full=False, firsts=firsts, folds=[]))
    while not place_folds(sets, ctx_count, reach):
        pass
    return sorted(sets, key=lambda entry: not entry["full"])


def place_folds(sets, ctx_count, reach):
    for entry in sets:
        entry["folds"] = []
    for entry in sets:
        offset = entry["offset"]
        for b in entry["firsts"]:
            if entry["full"] or 2 * b < 2 * ctx_count - 1 - reach - offset:
                continue
            for other in sets:
                busy = [x for f in other["firsts"] for x in (f, f + other["offset"])]
                busy += [x for pair in other["folds"] for x in pair]
                sends_low = ((b + offset) // other["offset"]) % 2 == other["colour"]
                if b not in busy and b + offset not in busy and sends_low and not other["full"]:
                    other["folds"].append((b, b + offset))
                    break
            else:
                entry["full"] = True
                return False
    return True


def key_of(entry):
    return entry["offset"], entry["colour"]


def swap(value, exchange, ctx_count, head_count):
    partner = {}
    pairs = [(b, b + exchange["offset"]) for b in exchange["firsts"]] + exchange["folds"]
    for a, b in pairs:
        partner[a], partner[b] = b, a
    pairs = []
    for b in range(ctx_count):
        for h in range(head_count):
            if b in partner:
                pairs.append((b * head_count + h, partner[b] * head_count + h))
            else:
                pairs.append((b * head_count + h, b * head_count + (h + 1) % head_count))
    return lax.ppermute(value, ("ctx", "head"), pairs)


def fold_offsets(slot):
    return range(-(slot - 1), slot, 2)


def pack_kernel(sets, k_hbm, v_hbm, *refs):
    outs, sems = refs[: len(sets)], refs[len(sets)]
    me = lax.axis_index("ctx")
    length = k_hbm.shape[0] // 2
    width = k_hbm.shape[1]
    copies = []
    for i, (entry, out) in enumerate(zip(sets, outs)):
        first = (me // entry["offset"]) % 2 == entry["colour"]
        rows = pl.ds(pl.multiple_of(jnp.where(first, 0, length), length), length)
        for a, hbm in enumerate((k_hbm, v_hbm)):
            src = hbm if entry["full"] else hbm.at[rows, :]
            cols = slice(a * width, (a + 1) * width)
            copies.append(pltpu.make_async_copy(src, out.at[:, cols], sems.at[i, a]))
    for copy in copies:
        copy.start()
    for copy in copies:
        copy.wait()


def stage_kernel(
    ctx_count, docs_hbm, q_hbm, g_hbm, k_hbm, v_hbm, q_all, g_all, mine, bias, docs_ref, sems
):
    length = q_hbm.shape[0] // 2
    heads, _, width = q_all.shape
    lengths = pltpu.make_async_copy(docs_hbm, docs_ref, sems.at[2, 0])
    lengths.start()
    copies = [
        pltpu.make_async_copy(k_hbm, mine.at[:, :width], sems.at[2, 1]),
        pltpu.make_async_copy(v_hbm, mine.at[:, width:], sems.at[2, 2]),
    ]
    for h in range(heads):
        cols = slice(h * width, (h + 1) * width)
        for a, (src, dst) in enumerate(((q_hbm, q_all), (g_hbm, g_all))):
            copies.append(pltpu.make_async_copy(src.at[:, cols], dst.at[h], sems.at[a, h]))
    for copy in copies:
        copy.start()
    lengths.wait()
    me = lax.axis_index("ctx")
    merged = bias.shape[2]
    row = lax.broadcasted_iota(jnp.int32, (merged, length), 0)
    half = length // 2
    col = lax.broadcasted_iota(jnp.int32, (1, length), 1) % half
    for s, u in ((0, 0), (0, 1), (1, 0), (1, 1)):
        stretch = me if s == 0 else 2 * ctx_count - 1 - me
        q_pos = stretch * length + u * half + col
        start = jnp.int32(0)
        doc_start = jnp.zeros((1, length), jnp.int32)
        for i in range(docs_ref.shape[0]):
            doc_start = jnp.where(q_pos >= start, start, doc_start)
            start = start + docs_ref[i]
        k_pos = row + (stretch - 2 * (row // length)) * length
        k_pos = jnp.where(k_pos > q_pos, k_pos - merged, k_pos)
        bias[s, u] = jnp.where(k_pos >= doc_start, 0.0, MASKED)
    for copy in copies:
        copy.wait()


def stacked(ref, s, u, first=0, last=None):
    half = ref.shape[1] // 4
    start = (2 * s + u) * half
    return ref[first:last, start : start + half, :].reshape(-1, ref.shape[2])


def unfolded(ref, s, h, near_low):
    length = ref.shape[3]
    value = ref[s, h]
    own = value[:length, :] * near_low
    return jnp.concatenate([own, value[length:, :], value[:length, :] - own], axis=0)


def score_kernel(sets, ctx_count, reach, bias, q_all, g_all, mine, *refs):
    count = len(sets)
    recs = {key_of(s): (r, s["full"]) for s, r in zip(sets, refs[:count])}
    pb, dsb, kv_win, own_ref = refs[count : count + 4]
    send_refs = refs[count + 4 : 2 * count + 4]
    acc, extra = refs[2 * count + 4 :]
    me = lax.axis_index("ctx")
    length = mine.shape[0] // 2
    width = HEAD_DIM
    heads = q_all.shape[0]
    merged = reach * length
    scaling = width ** (-0.5)
    log_scale = scaling * math.log2(math.e)

    def low_part(key):
        ref, full = recs[key]
        return ref[:length, :] if full else ref[...]

    def up_part(key):
        ref, full = recs[key]
        return ref[length:, :] if full else ref[...]

    def pick(part, offset, colour_pred):
        have = [c for c in range(2) if (offset, c) in recs]
        if len(have) == 1:
            return part((offset, have[0]))
        return jnp.where(colour_pred, part((offset, 1)), part((offset, 0)))

    lows = [mine[:length, :]]
    highs = [mine[length:, :]]
    for slot in range(1, reach + 1):
        odd = (me // slot) % 2 == 1
        lows.append(pick(low_part, slot, jnp.logical_not(odd)))
        highs.append(pick(up_part, slot, odd))
    for slot in range(1, reach + 1):
        folded = me + slot >= ctx_count
        value = highs[slot]
        for offset in fold_offsets(slot):
            here = folded & (2 * ctx_count - 1 - 2 * me - slot == offset)
            if offset <= 0:
                value = jnp.where(here, lows[-offset], value)
            else:
                for colour in range(2):
                    if recs.get((offset, colour), (None, False))[1]:
                        where = here & ((me // offset) % 2 == colour)
                        value = jnp.where(where, low_part((offset, colour)), value)
                for entry in sets:
                    for pair in entry["folds"]:
                        if pair[1] - pair[0] == offset:
                            where = here & (me == pair[0])
                            value = jnp.where(where, recs[key_of(entry)][0][...], value)
        highs[slot] = value
    for slot in range(reach + 1):
        rows = slice(slot * length, (slot + 1) * length)
        kv_win[0, rows, :] = lows[slot]
        kv_win[1, rows, :] = highs[slot]

    half = length // 2
    group = next(g for g in (4, 2) if heads % g == 0)
    lanes = 2 * half
    tri_row = lax.broadcasted_iota(jnp.int32, (half, lanes), 0)
    near = tri_row <= lax.broadcasted_iota(jnp.int32, (half, lanes), 1) % half
    far_low = jnp.where(near, 0.0, 1.0).astype(jnp.bfloat16)
    contract_last = (((1,), (1,)), ((), ()))

    def products(s, u, h):
        own_rows = slice(0, length if u else half)
        last_rows = slice(merged + half if u else merged, None)

        def window(cols):
            parts = [kv_win[s, own_rows, cols], kv_win[s, length:merged, cols]]
            return jnp.concatenate(parts + [kv_win[s, last_rows, cols]], axis=0)

        raw = lax.dot_general(
            window(slice(0, width)),
            stacked(q_all, s, u, h, h + group),
            contract_last,
            preferred_element_type=jnp.float32,
        )
        d_p = lax.dot_general(
            window(slice(width, None)),
            stacked(g_all, s, u, h, h + group),
            contract_last,
            preferred_element_type=jnp.float32,
        )
        return raw, d_p

    def fold(u, value):
        if u:
            top = value[:half, :]
            low = jnp.where(near, value[half:length, :], value[merged:, :])
            middle = value[length:merged, :]
        else:
            last = value[merged - half :, :]
            top = jnp.where(near, value[:half, :], last[:half, :])
            low = last[half:, :]
            middle = value[half : merged - half, :]
        return jnp.concatenate([top, low, middle], axis=0)

    def soften(s, u, block, raw, d_p):
        raw = fold(u, raw) + bias[s, u]
        d_p = fold(u, d_p)
        top = jnp.max(raw, axis=0, keepdims=True)
        weight = jnp.exp2((raw - top) * log_scale)
        total = jnp.sum(weight, axis=0, keepdims=True)
        inverse = 1.0 / total
        delta = jnp.sum(weight * d_p, axis=0, keepdims=True) * inverse
        weight = weight * inverse
        others = []
        for ref, value in ((pb, weight), (dsb, weight * (d_p - delta))):
            value = value.astype(jnp.bfloat16)
            ref[s, block] = value
            if u:
                last = [value[half:length, :] * far_low]
            else:
                last = [value[:half, :] * far_low, value[half:length, :]]
            others.append(jnp.concatenate([value[length:, :]] + last, axis=0))
        return others

    def gradients(s, u, first, last, start, done):
        weights, d_scores = [jnp.concatenate(values, axis=1) for values in zip(*done)]
        parts = [(slice(length, merged), slice(0, merged - length))] if merged > length else []
        parts.append((slice(merged + u * half, merged + length), slice(merged - length, None)))
        for cols, left, right in (
            (slice(0, width), d_scores, q_all),
            (slice(width, None), weights, g_all),
        ):
            value = jnp.dot(
                left, stacked(right, s, u, first, last), preferred_element_type=jnp.float32
            )
            if right is q_all:
                value = value * scaling
            for rows, part in parts:
                if start:
                    acc[s, rows, cols] = value[part, :]
                else:
                    acc[s, rows, cols] = acc[s, rows, cols] + value[part, :]

    items = [(s, u, h) for s in range(2) for u in range(2) for h in range(0, heads, group)]
    done = []
    ready = products(*items[0])
    for i, (s, u, h) in enumerate(items):
        following = products(*items[i + 1]) if i + 1 < len(items) else None
        for j in range(0, group, 2):
            part = slice(j // 2 * lanes, (j // 2 + 1) * lanes)
            block = (u * heads + h + j) // 2
            done.append(soften(s, u, block, ready[0][:, part], ready[1][:, part]))
        ready = following
        last = h + group
        if last == heads or (s, u) == (1, 1) and last == heads - group:
            first = last - 2 * len(done)
            gradients(s, u, first, last, u == 0, done)
            done = []

    def slot_rows(slot):
        return slice(slot * length, (slot + 1) * length)

    extra[...] = jnp.zeros(extra.shape, jnp.float32)
    for slot in range(1, reach + 1):
        for offset in fold_offsets(slot):

            @pl.when((me + slot >= ctx_count) & (2 * ctx_count - 1 - 2 * me - slot == offset))
            def _():
                part = acc[1, slot_rows(slot), :]
                if offset < 0:
                    acc[0, slot_rows(-offset), :] = acc[0, slot_rows(-offset), :] + part
                else:
                    extra[slot_rows(offset), :] = part

    own_ref[...] = extra[:length, :]
    for entry, ref in zip(sets, send_refs):
        offset = entry["offset"]
        first = (me // offset) % 2 == entry["colour"]
        side = jnp.where(first, 1, 0)
        if entry["full"]:
            to_low = acc[0, slot_rows(offset), :]
            to_up = acc[1, slot_rows(offset), :]
            more = extra[slot_rows(offset), :]
            ref[:length, :] = jnp.where(first, more, to_low).astype(jnp.bfloat16)
            ref[length:, :] = jnp.where(first, to_up, 0.0).astype(jnp.bfloat16)
        else:
            part = acc[side, slot_rows(offset), :]
            for pair in entry["folds"]:
                part = jnp.where(me == pair[0], extra[slot_rows(pair[1] - pair[0]), :], part)
            ref[...] = part.astype(jnp.bfloat16)


def output_kernel(pb, dsb, kv_win, q_all, g_all, att_hbm, dq_hbm, own_ref, att, dq, sems):
    length = att.shape[0] // 2
    width = HEAD_DIM
    heads = att.shape[1] // width
    scaling = width ** (-0.5)
    group = next(g for g in (4, 2) if heads % g == 0)
    half = length // 2
    tri_row = lax.broadcasted_iota(jnp.int32, (length, 2 * half), 0)
    tri_col = lax.broadcasted_iota(jnp.int32, (length, 2 * half), 1) % half
    copies = []
    for s in range(2):
        k_turn = kv_win[s, :, :width].T
        v_turn = kv_win[s, :, width:].T
        own_weights, own_scores = [], []
        for u in range(2):
            near_low = jnp.where(tri_row <= tri_col + u * half, 1.0, 0.0).astype(jnp.bfloat16)
            for h in range(0, heads, group):
                blocks = [(u * heads + h + j) // 2 for j in range(0, group, 2)]
                weights = [unfolded(pb, s, block, near_low) for block in blocks]
                d_scores = [unfolded(dsb, s, block, near_low) for block in blocks]
                own_weights += [value[:length, :] for value in weights]
                own_scores += [value[:length, :] for value in d_scores]
                out_t = jnp.dot(
                    v_turn, jnp.concatenate(weights, axis=1), preferred_element_type=jnp.float32
                )
                dq_t = jnp.dot(
                    k_turn, jnp.concatenate(d_scores, axis=1), preferred_element_type=jnp.float32
                )
                out_t = out_t.astype(jnp.bfloat16)
                dq_t = (dq_t * scaling).astype(jnp.bfloat16)
                rows = slice((2 * s + u) * half, (2 * s + u + 1) * half)
                for j in range(0, group, 2):
                    part = slice(j * half, (j + 2) * half)
                    for ref, value in ((att, out_t[:, part].T), (dq, dq_t[:, part].T)):
                        for i in range(2):
                            cols = slice((h + j + i) * width, (h + j + i + 1) * width)
                            ref[rows, cols] = value[i * half : (i + 1) * half, :]
        rows = slice(s * length, (s + 1) * length)
        for a, (src, dst) in enumerate(((att, att_hbm), (dq, dq_hbm))):
            copy = pltpu.make_async_copy(src.at[rows, :], dst.at[rows, :], sems.at[s, a])
            copy.start()
            copies.append(copy)
        d_k = jnp.dot(
            jnp.concatenate(own_scores, axis=1),
            jnp.concatenate([stacked(q_all, s, u) for u in range(2)], axis=0),
            preferred_element_type=jnp.float32,
        )
        d_v = jnp.dot(
            jnp.concatenate(own_weights, axis=1),
            jnp.concatenate([stacked(g_all, s, u) for u in range(2)], axis=0),
            preferred_element_type=jnp.float32,
        )
        own_ref[rows, :width] = d_k * scaling
        own_ref[rows, width:] = d_v
    for copy in copies:
        copy.wait()


def sum_kernel(sets, ctx_count, own_ref, fold_ref, *refs):
    dk_hbm, dv_hbm, dk, dv, sems = refs[len(sets) :]
    me = lax.axis_index("ctx")
    length = own_ref.shape[0] // 2
    width = dk.shape[1]
    copies = []
    for a, (stage, hbm) in enumerate(((dk, dk_hbm), (dv, dv_hbm))):
        cols = slice(a * width, (a + 1) * width)
        low = own_ref[:length, cols] + fold_ref[:, cols]
        up = own_ref[length:, cols]
        for entry, ref in zip(sets, refs):
            offset = entry["offset"]
            first = (me // offset) % 2 == entry["colour"]
            as_first = first & (me + offset < ctx_count)
            as_second = jnp.logical_not(first) & (me >= offset)
            if entry["full"]:
                to_low = ref[:length, cols].astype(jnp.float32)
                low = low + jnp.where(as_first | as_second, to_low, 0.0)
                up = up + jnp.where(as_second, ref[length:, cols].astype(jnp.float32), 0.0)
            else:
                part = ref[:, cols].astype(jnp.float32)
                for pair in entry["folds"]:
                    as_first = as_first & (me != pair[0]) | (me == pair[1])
                low = low + jnp.where(as_first, part, 0.0)
                up = up + jnp.where(as_second, part, 0.0)
        stage[:length, :] = low.astype(jnp.bfloat16)
        stage[length:, :] = up.astype(jnp.bfloat16)
        copy = pltpu.make_async_copy(stage, hbm, sems.at[a])
        copy.start()
        copies.append(copy)
    for copy in copies:
        copy.wait()


def in_vmem(amount):
    return [pl.BlockSpec(memory_space=pltpu.VMEM)] * amount


def in_place(amount):
    return [pl.BlockSpec(memory_space=pl.ANY)] * amount


def on_chip(values):
    return [pltpu.with_memory_space_constraint(v, pltpu.VMEM) for v in values]


def off_chip(values):
    return [pltpu.with_memory_space_constraint(v, pltpu.HBM) for v in values]


def attention(query_rows, key_rows, value_rows, out_grad, doc_lengths):
    ctx_count = lax.axis_size("ctx")
    head_count = lax.axis_size("head")
    tok_dev = query_rows.shape[0]
    length = tok_dev // 2
    width = key_rows.shape[1]
    reach = min(DOC_STRETCHES, ctx_count // 4)
    span = (reach + 1) * length
    heads = query_rows.shape[1] // width
    sets = exchanges(ctx_count, reach)
    count = len(sets)
    payloads = [
        pltpu.VMEM((2 * length if s["full"] else length, 2 * width), jnp.bfloat16) for s in sets
    ]
    keys_values = off_chip([key_rows, value_rows])
    packed = pl.pallas_call(
        lambda *refs: pack_kernel(sets, *refs),
        out_shape=payloads,
        in_specs=in_place(2),
        out_specs=in_vmem(count),
        scratch_shapes=[pltpu.SemaphoreType.DMA((count, 2))],
        compiler_params=pltpu.CompilerParams(vmem_limit_bytes=VMEM_LIMIT),
        name="pack",
    )(*keys_values)
    received = [swap(p, s, ctx_count, head_count) for p, s in zip(packed, sets)]

    stack = pltpu.VMEM((heads, tok_dev, width), jnp.bfloat16)
    q_all, g_all, mine, bias = pl.pallas_call(
        lambda *refs: stage_kernel(ctx_count, *refs),
        out_shape=[
            stack,
            stack,
            pltpu.VMEM((tok_dev, 2 * width), jnp.bfloat16),
            pltpu.VMEM((2, 2, reach * length, length), jnp.float32),
        ],
        in_specs=in_place(5),
        out_specs=in_vmem(4),
        scratch_shapes=[
            pltpu.SMEM(doc_lengths.shape, jnp.int32),
            pltpu.SemaphoreType.DMA((3, heads)),
        ],
        compiler_params=pltpu.CompilerParams(vmem_limit_bytes=VMEM_LIMIT),
        name="stage",
    )(*off_chip([doc_lengths, query_rows, out_grad]), *keys_values)

    low_weights = pltpu.VMEM((2, heads, reach * length, length), jnp.bfloat16)
    pb, dsb, kv_win, folded, *partials = pl.pallas_call(
        lambda *refs: score_kernel(sets, ctx_count, reach, *refs),
        out_shape=[
            low_weights,
            low_weights,
            pltpu.VMEM((2, span, 2 * width), jnp.bfloat16),
            pltpu.VMEM((length, 2 * width), jnp.float32),
        ]
        + payloads,
        in_specs=in_vmem(4 + count),
        out_specs=in_vmem(4 + count),
        scratch_shapes=[
            pltpu.VMEM((2, span, 2 * width), jnp.float32),
            pltpu.VMEM((reach * length, 2 * width), jnp.float32),
        ],
        compiler_params=pltpu.CompilerParams(vmem_limit_bytes=VMEM_LIMIT),
        name="score",
    )(*on_chip([bias, q_all, g_all, mine, *received]))
    returned = [swap(p, s, ctx_count, head_count) for p, s in zip(partials, sets)]

    attended, query_grad, own = pl.pallas_call(
        output_kernel,
        out_shape=[jax.ShapeDtypeStruct(query_rows.shape, jnp.bfloat16)] * 2
        + [pltpu.VMEM((tok_dev, 2 * width), jnp.float32)],
        in_specs=in_vmem(5),
        out_specs=in_place(2) + in_vmem(1),
        scratch_shapes=[
            pltpu.VMEM(query_rows.shape, jnp.bfloat16),
            pltpu.VMEM(query_rows.shape, jnp.bfloat16),
            pltpu.SemaphoreType.DMA((2, 2)),
        ],
        compiler_params=pltpu.CompilerParams(vmem_limit_bytes=VMEM_LIMIT),
        name="output",
    )(*on_chip([pb, dsb, kv_win, q_all, g_all]))

    key_grad, value_grad = pl.pallas_call(
        lambda *refs: sum_kernel(sets, ctx_count, *refs),
        out_shape=[jax.ShapeDtypeStruct(key_rows.shape, jnp.bfloat16)] * 2,
        in_specs=in_vmem(2 + count),
        out_specs=in_place(2),
        scratch_shapes=[pltpu.VMEM(key_rows.shape, jnp.bfloat16)] * 2
        + [pltpu.SemaphoreType.DMA((2,))],
        compiler_params=pltpu.CompilerParams(vmem_limit_bytes=VMEM_LIMIT),
        name="total",
    )(*on_chip([own, folded, *returned]))
    return (attended, query_grad, key_grad, value_grad)


def solution(mesh):
    placed = (
        P(("groups", "ctx"), "head"),
        P(("groups", "ctx"), "head"),
        P(("groups", "ctx"), "head"),
        P(("groups", "ctx"), "head"),
        P("groups"),
    )
    return jax.shard_map(
        attention,
        mesh=mesh,
        in_specs=placed,
        out_specs=(P(("groups", "ctx"), "head"),) * 4,
        check_vma=False,
    )
```
